512 devices in a mesh: gx: 4 (over z_hi, core), gy: 8 (over z_lo), gz: 16 (over x, y).
Axes of the slice: x: 4, y: 4, z: 16 (z_hi: 2, z_lo: 8; z = z_hi * 8 + z_lo), core: 2. Of those that a mesh axis runs over, the one named last changes fastest.
Arguments:
- right_side: float32 [32, 128, 2048], P('gx', 'gy', 'gz'), may hold values from -8 to 8
- coefficient: float32 [32, 128, 2048], P('gx', 'gy', 'gz'), may hold values from 0.05 to 2
Outputs:
- correction: float32 [32, 128, 2048], P('gx', 'gy', 'gz')
The draws below stay inside these ranges and needn't reach their ends.
All inputs are finite; a program needn't handle non-finite values.
Results may differ from the reference program's by a relative error of at most 0.00002.
Values sent between devices are 32-bit elements; how exact they have to be, the bound alone decides.
No kernel may reach another device: no remote copies, remote signals or barrier semaphores. Data moves between devices by JAX's collectives and lax.ppermute only.
A program may use at most 64 MiB of HBM per device.

```python
import math
import jax
import jax.numpy as jnp

SWEEPS = 4
NX = 32
NY = 128
NZ = 2048


def level_of(key, extent, cuts, low, top_value):
    def one(dim, blocks):
        steps = jax.random.uniform(jax.random.fold_in(jax.random.fold_in(key, 6), dim), (blocks,), jnp.float32, low / len(cuts), top_value / len(cuts))
        return jnp.repeat(jnp.exp(steps), extent[dim] // blocks).reshape((-1,) + (1,) * (len(extent) - dim - 1))

    factor_of = one(*cuts[0])
    for cut in cuts[1:]:
        factor_of = factor_of * one(*cut)
    return factor_of


def centred(key, shape, deviation, limit, shards=(), held_as=jnp.bfloat16):
    factor_of = level_of(key, shape, shards, -0.22, 0.18) if shards else 1.0
    array = jax.random.normal(key, shape, jnp.float32) * deviation * factor_of
    return jnp.minimum(jnp.maximum(array, -limit), limit).astype(held_as)


def setup_inputs(seed: int = 0) -> dict:
    keys = jax.random.split(jax.random.key(seed), 3)
    return {
        "right_side": centred(keys[0], (NX, NY, NZ), 3.0, 8.0, ((0, 4), (1, 8), (2, 16)), jnp.float32),
        "coefficient": jnp.clip(jnp.exp(math.log(2.0) - 3.6888794 * jax.random.uniform(keys[1], (NX, NY, NZ), jnp.float32) ** level_of(keys[1], (NX, NY, NZ), ((0, 4), (1, 8), (2, 16)), -0.2, 0.2)), 0.05, 2.0),
    }


RELAX_WEIGHT = 0.8


def restrict(values):
    return values.reshape(values.shape[0] // 2, 2, values.shape[1] // 2, 2, values.shape[2] // 2, 2).mean(axis=(1, 3, 5))


def prolong(values):
    return jnp.repeat(jnp.repeat(jnp.repeat(values, 2, axis=0), 2, axis=1), 2, axis=2)


def neighbours(padded):
    beside_all = padded[2:, 1:-1, 1:-1] + padded[:-2, 1:-1, 1:-1]
    beside_all = beside_all + padded[1:-1, 2:, 1:-1] + padded[1:-1, :-2, 1:-1]
    return beside_all + padded[1:-1, 1:-1, 2:] + padded[1:-1, 1:-1, :-2]


def smooth(residual, coefficient, spacing_scale):
    diagonal = 6.0 * spacing_scale + coefficient
    iterate = RELAX_WEIGHT * residual / diagonal
    for repeat in range(SWEEPS - 1):
        beside_all = neighbours(jnp.pad(iterate, 1))
        iterate = iterate + RELAX_WEIGHT * (residual - (diagonal * iterate - spacing_scale * beside_all)) / diagonal
    return iterate


def plane_term(residual, coefficient):
    return jnp.mean(residual, axis=(0, 1)) / jnp.mean(coefficient + 0.0625, axis=(0, 1))


def reference(right_side, coefficient):
    residual_one = restrict(right_side)
    coeff_one = restrict(coefficient)
    residual_two = restrict(residual_one)
    coeff_two = restrict(coeff_one)
    correction_two = smooth(residual_two, coeff_two, 0.0625) + plane_term(residual_two, coeff_two)[None, None, :]
    correction_one = smooth(residual_one, coeff_one, 0.25) + prolong(correction_two)
    return smooth(right_side, coefficient, 1.0) + prolong(correction_one)
```

```python
import functools
import itertools

import jax
import jax.numpy as jnp
from jax import lax
from jax.experimental import pallas as pl
from jax.experimental.pallas import tpu as pltpu
from jax.sharding import PartitionSpec as P

SWEEPS = 4
RELAX = 0.8
KEEP = 1.0 - RELAX
F32 = jnp.float32
VMEM = pl.BlockSpec(memory_space=pltpu.VMEM)
HIGHEST = lax.Precision.HIGHEST
AXES = ("gx", "gy", "gz")


def even_groups(nx, ny, nz):
    groups = []
    for gx, ya, za in itertools.product(range(nx), range(0, ny, 2), range(0, nz, 2)):
        groups.append([(gx * ny + ya + a) * nz + za + b for a in (0, 1) for b in (0, 1)])
    return groups


def odd_groups(nx, ny, nz):
    groups = []
    for gx in range(nx):
        flat = lambda gy, gz: (gx * ny + gy) * nz + gz % nz
        for ya, za in itertools.product(range(1, ny - 1, 2), range(1, nz, 2)):
            groups.append([flat(ya + a, za + b) for a in (0, 1) for b in (0, 1)])
        for gy, za in itertools.product((0, ny - 1), range(1, nz, 4)):
            groups.append([flat(gy, za + 2 * a + b) for a in (0, 1) for b in (0, 1)])
    return groups


def spots(ny, nz):
    gx, gy, gz = (lax.axis_index(a) for a in AXES)
    one = 2 * (gy & 1) + (gz & 1)
    inner = (gy > 0) & (gy < ny - 1)
    half = jnp.where(inner, (gy + 1) & 1, ((gz + nz - 1) & (nz - 1)) // 2 & 1)
    two = 2 * half + ((gz + 1) & 1)
    return gx, gy, gz, one, two, inner


def lanes(shape=(8, 128)):
    return lax.broadcasted_iota(jnp.int32, shape, len(shape) - 1)


def rows(shape=(8, 128)):
    return lax.broadcasted_iota(jnp.int32, shape, len(shape) - 2)


def turn(x, shift, axis):
    shift = shift % x.shape[axis]
    return pltpu.roll(x, shift, axis) if shift else x


def first_kernel(nx, r_ref, c_ref, x_ref, v_ref, w_ref, v1_ref, w1_ref, v2_ref, w2_ref, s_ref, t_ref, u_ref, d_ref):
    gx = lax.axis_index("gx")
    r, c = r_ref[...], c_ref[...]
    w = RELAX / (6.0 + c)
    v = w * r
    v_ref[...] = v
    w_ref[...] = w
    r4, c4 = r.reshape(4, 2, 16, 128), c.reshape(4, 2, 16, 128)
    t_ref[0:4] = r4[:, 0] + r4[:, 1]
    t_ref[4:8] = c4[:, 0] + c4[:, 1]
    a = t_ref[:, pl.ds(0, 8, stride=2), :] + t_ref[:, pl.ds(1, 8, stride=2), :]
    src, dst = rows((128, 128)), lanes((128, 128))
    half = jnp.where((src >> 1) == (dst & 63), 0.125, 0.0).astype(F32)
    one = jnp.dot(a.reshape(64, 128), half, precision=HIGHEST, preferred_element_type=F32)
    r1, c1 = one[:32].reshape(4, 8, 128), one[32:].reshape(4, 8, 128)
    d1 = RELAX / (1.5 + c1)
    v1, w1 = d1 * r1, d1 * 0.25
    v1_ref[...] = v1
    w1_ref[...] = w1
    a4 = a.reshape(4, 2, 8, 128)
    u_ref[...] = a4[:, 0] + a4[:, 1]
    e = u_ref[:, pl.ds(0, 4, stride=2), :] + u_ref[:, pl.ds(1, 4, stride=2), :]
    d_ref[:, 0:4, :] = e
    d_ref[:, 4:8, :] = e
    quarter = jnp.where((src >> 2) == (dst & 31), 0.015625, 0.0).astype(F32)
    two = jnp.dot(d_ref[...].reshape(32, 128), quarter, precision=HIGHEST, preferred_element_type=F32)
    r2, c2 = two[:16].reshape(2, 8, 128), two[16:].reshape(2, 8, 128)
    d2 = RELAX / (0.375 + c2)
    v2, w2 = d2 * r2, d2 * 0.0625
    v2_ref[...] = v2
    w2_ref[...] = w2
    lane, row = lanes(), rows()
    low = lane < 64
    sums = jnp.where(low, r2[0] + r2[1], c2[0] + c2[1])
    s_ref[...] = 0.5 * jnp.sum(sums, axis=0, keepdims=True)
    quad = (lane & 63) < 32
    both = [jnp.where(quad, v2[i], w2[i]) for i in (0, 1)]
    last = jnp.where(row < 4, both[0], both[1])
    for j in range(nx):
        up = j > gx
        for d in range(3):
            face = jnp.where(up, v[7 - d], v[d])
            x_ref[j, 2 * d] = face[0:8]
            x_ref[j, 2 * d + 1] = face[8:16]
        for d in range(2):
            face = jnp.where(up, w[7 - d], w[d])
            x_ref[j, 6 + 2 * d] = face[0:8]
            x_ref[j, 7 + 2 * d] = face[8:16]
        for d in range(3):
            x_ref[j, 10 + d] = jnp.where(low, jnp.where(up, v1[3 - d], v1[d]), jnp.where(up, w1[3 - d], w1[d]))
        x_ref[j, 13] = last


def extended(nx, gx, v_ref, w_ref, v1_ref, w1_ref, v2_ref, w2_ref, x_ref):
    lane, row = lanes(), rows()
    low = lane < 64
    quad = (lane & 63) < 32
    left, right = jnp.maximum(gx - 1, 0), jnp.minimum(gx + 1, nx - 1)
    far_left, far_right = jnp.maximum(gx - 2, 0), jnp.minimum(gx + 2, nx - 1)
    has_left, has_right = gx > 0, gx < nx - 1
    has_far_left, has_far_right = gx > 1, gx < nx - 2

    def pick(slot, tile, have):
        return jnp.where(have, x_ref[slot, tile], 0.0)

    def pair(slot, tile, have):
        return jnp.concatenate([pick(slot, tile, have), pick(slot, tile + 1, have)], axis=0)

    def fine(slot, d, have):
        return pair(slot, 2 * d, have), (pair(slot, 6 + 2 * d, have) if d < 2 else None)

    def middle(slot, d, have):
        t = pick(slot, 10 + d, have)
        s = turn(t, 64, 1)
        return jnp.where(low, t, s), jnp.where(low, s, t)

    def coarse(slot, layer, have):
        t = pick(slot, 13, have)
        s = turn(t, 4, 0)
        t = jnp.where(row < 4, t, s) if layer == 0 else jnp.where(row < 4, s, t)
        s = turn(t, 32, 1)
        return jnp.where(quad, t, s), jnp.where(quad, s, t)

    level0 = (
        [fine(left, d, has_left) for d in (2, 1, 0)]
        + [(v_ref[i], w_ref[i]) for i in range(8)]
        + [fine(right, d, has_right) for d in (0, 1, 2)]
    )
    level1 = (
        [middle(left, d, has_left) for d in (2, 1, 0)]
        + [(v1_ref[i], w1_ref[i]) for i in range(4)]
        + [middle(right, d, has_right) for d in (0, 1, 2)]
    )
    level2 = (
        [coarse(far_left, 1, has_far_left), coarse(left, 0, has_left), coarse(left, 1, has_left)]
        + [(v2_ref[i], w2_ref[i]) for i in range(2)]
        + [coarse(right, 0, has_right), coarse(right, 1, has_right), coarse(far_right, 0, has_far_right)]
    )
    return level0, level1, level2


def edge_lanes(layers):
    shape = layers[0][0].shape
    lane = lanes(shape)
    packed = jnp.zeros(shape, F32)
    for k, (v, w) in enumerate(layers):
        at = 10 * k
        packed = jnp.where((lane >= at) & (lane < at + 6), turn(v, at + 3, 1), packed)
        packed = jnp.where((lane >= at + 6) & (lane < at + 10), turn(w, at + 8, 1), packed)
    return packed


def second_kernel(nx, ny, nz, v_ref, w_ref, v1_ref, w1_ref, v2_ref, w2_ref, x_ref, one_ref, two_ref):
    gx, gy, gz, one, two, _ = spots(ny, nz)
    level0, level1, level2 = extended(nx, gx, v_ref, w_ref, v1_ref, w1_ref, v2_ref, w2_ref, x_ref)
    lane, row = lanes(), rows()
    low = lane < 64
    quad = (lane & 63) < 32
    up = (gy & 1) == 0
    ends = [edge_lanes(level0[1:13])]
    ends = [ends[0][0:8], ends[0][8:16], edge_lanes(level1[1:9]), edge_lanes(level2[1:7])]
    for i, tile in enumerate(ends):
        for slot in (one ^ 1, one ^ 2, one ^ 3):
            one_ref[slot, 12 + i] = tile
        for slot in (two ^ 1, two ^ 3):
            two_ref[slot, i] = tile
    for k in range(12):
        v, w = level0[k + 1]
        if k < 8:
            a, b = level1[k + 1]
            extra = jnp.where(low, a, b)
        elif k < 11:
            a, b = (jnp.where(quad, *level2[1 + 2 * (k - 8) + i]) for i in (0, 1))
            extra = jnp.where(low, a, b)
        else:
            extra = jnp.zeros((8, 128), F32)
        high = jnp.where(row >= 5, v[8:16], jnp.where(row >= 3, turn(w[8:16], 5, 0), turn(extra, 3, 0)))
        base = jnp.where(row < 3, v[0:8], jnp.where(row < 5, turn(w[0:8], 3, 0), turn(extra, 5, 0)))
        one_ref[one ^ 2, k] = jnp.where(up, high, base)
        two_ref[two ^ 2, k] = jnp.where(up, base, high)


def forward_kernel(ny, nz, got_ref, old_ref, two_ref):
    _, _, _, one, two, _ = spots(ny, nz)
    two_ref[...] = old_ref[...]
    for i in range(4):
        two_ref[two ^ 2, 12 + i] = got_ref[one ^ 1, 12 + i]
        two_ref[two ^ 1, 12 + i] = got_ref[one ^ 2, 12 + i]


def around(v, above, below):
    return (
        above
        + below
        + turn(v, 1, 0)
        + turn(v, -1, 0)
        + turn(v, 1, 1)
        + turn(v, -1, 1)
    )


def relaxed(v_ref, w_ref, a_ref, b_ref, count):
    done = []
    for sweep in range(SWEEPS - 1):
        source = (v_ref, a_ref, b_ref)[sweep]
        target = (a_ref, b_ref, None)[sweep]
        for i in range(sweep + 1, count - sweep - 1):
            v = source[i]
            new = KEEP * v + v_ref[i] + w_ref[i] * around(v, source[i - 1], source[i + 1])
            if target is None:
                done.append(new)
            else:
                target[i] = new
    return done


def last_kernel(
    nx, ny, nz, v_ref, w_ref, v1_ref, w1_ref, v2_ref, w2_ref, x_ref, one_ref, two_ref, plane_ref, out_ref,
    fv, fw, fa, fb, mv, mw, ma, mb, cv, cw, ca, cb, wide_ref, deep_ref,
):
    gx, gy, gz, one, two, has_y = spots(ny, nz)
    has_z = (gz > 0) & (gz < nz - 1)
    up = (gy & 1) == 0
    ahead = (gz & 1) == 0
    level0, level1, level2 = extended(nx, gx, v_ref, w_ref, v1_ref, w1_ref, v2_ref, w2_ref, x_ref)
    lane, row = lanes(), rows()
    part = lane - 10 * (lane // 10)
    first_half = (part < 3) | ((part >= 6) & (part < 8))
    from_one = jnp.where(ahead, jnp.where(first_half, 0, 1), jnp.where(first_half, 1, 0)) == 1

    own, plus, minus = [], [], []
    for i in range(4):
        z_two = jnp.where(has_z, two_ref[two ^ 1, i], 0.0)
        own.append(jnp.where(from_one, one_ref[one ^ 1, 12 + i], z_two))
        z_two = jnp.where(has_z, two_ref[two ^ 1, 12 + i], 0.0)
        t_one = jnp.where(from_one, one_ref[one ^ 3, 12 + i], z_two)
        z_two = jnp.where(has_z, two_ref[two ^ 3, i], 0.0)
        t_two = jnp.where(has_y, jnp.where(from_one, two_ref[two ^ 2, 12 + i], z_two), 0.0)
        plus.append(jnp.where(up, t_one, t_two))
        minus.append(jnp.where(up, t_two, t_one))
    none = jnp.zeros((8, 128), F32)

    def outer(p, m):
        return jnp.where(row < 3, p, jnp.where(row >= 5, m, none))

    z0 = jnp.concatenate([own[0], own[1], outer(plus[0], minus[1])], axis=0)
    z1 = jnp.concatenate([own[2], outer(plus[2], minus[2])], axis=0)
    z2 = jnp.concatenate([jnp.where(row < 4, own[3], plus[3]), jnp.where(row >= 5, minus[3], none)], axis=0)

    lane16 = lanes((16, 128))
    fv[0, 0:16, 0:128] = level0[0][0]
    fv[13, 0:16, 0:128] = level0[13][0]
    for i in (0, 13):
        fv[i, 16:24, 0:128] = none
        fv[i, :, 128:256] = jnp.zeros((24, 128), F32)
    for k in range(12):
        a = one_ref[one ^ 2, k]
        b = jnp.where(has_y, two_ref[two ^ 2, k], 0.0)
        p, m = jnp.where(up, a, b), jnp.where(up, b, a)
        v, w = level0[k + 1]
        fv[k + 1, 0:16, 0:128] = v
        fw[k + 1, 0:16, 0:128] = w
        fv[k + 1, 16:24, 0:128] = outer(p, m)
        fw[k + 1, 16:24, 0:128] = jnp.where(row < 2, turn(p, 5, 0), jnp.where(row >= 6, turn(m, 3, 0), none))
        fv[k + 1, :, 128:256] = turn(z0, -(10 * k + 3), 1)
        fw[k + 1, :, 128:256] = turn(z0, -(10 * k + 8), 1)
        if k < 8:
            extra = outer(turn(p, 3, 0), turn(m, 5, 0))
            v, w = level1[k + 1]
            v = jnp.concatenate([v, extra], axis=0)
            w = jnp.concatenate([w, turn(extra, 64, 1)], axis=0)
            at = 10 * k + 3
            mv[k + 1] = jnp.where(lane16 < 64, v, jnp.where(lane16 < 96, turn(z1, 64 - at, 1), turn(z1, -at, 1)))
            at = 10 * k + 8
            mw[k + 1] = jnp.where(lane16 < 64, w, jnp.where(lane16 < 96, turn(z1, 64 - at, 1), turn(z1, -at, 1)))
        elif k < 11:
            near, far = turn(p, 7, 0), turn(m, 5, 0)
            for i in (0, 1):
                j = 2 * (k - 8) + i
                v, w = level2[j + 1]
                for field, target in ((0, cv), (1, cw)):
                    shift = -(64 * i + 32 * field)
                    top = jnp.where(row < 4, (v, w)[field], turn(near, shift, 1))
                    full = jnp.concatenate([top, jnp.where(row >= 5, turn(far, shift, 1), none)], axis=0)
                    at = 10 * j + (3, 8)[field]
                    ends = jnp.where(lane16 < 64, turn(z2, 32 - at, 1), turn(z2, -at, 1))
                    target[j + 1] = jnp.where(lane16 < 32, full, ends)
    for i in (0, 9):
        mv[i, 0:8] = level1[i][0]
        mv[i, 8:16] = none
    for i in (0, 7):
        cv[i, 0:8] = level2[i][0]
        cv[i, 8:16] = none

    coarse = relaxed(cv, cw, ca, cb, 8)
    s = plane_ref[...]
    plane = jnp.where(lane < 64, s / (turn(jnp.broadcast_to(s, (8, 128)), 64, 1) + 16.0), 0.0)
    src, dst = rows((128, 128)), lanes((128, 128))
    spread4 = jnp.where(src == (dst >> 2), 1.0, 0.0).astype(F32)
    spread2 = jnp.where(src == (dst >> 1), 1.0, 0.0).astype(F32)
    c = jnp.concatenate([layer[0:8] + plane for layer in coarse], axis=0)
    c = jnp.dot(c, spread4, precision=HIGHEST, preferred_element_type=F32).reshape(2, 8, 128)
    middle = relaxed(mv, mw, ma, mb, 10)
    m = jnp.concatenate([layer[0:8] for layer in middle], axis=0)
    m = jnp.dot(m, spread2, precision=HIGHEST, preferred_element_type=F32).reshape(4, 8, 128)
    for i in range(2):
        for j in range(2):
            deep_ref[i, pl.ds(j, 4, stride=2), :] = c[i, 0:4]
    for i in range(4):
        total = m[i] + deep_ref[i // 2]
        for j in range(2):
            wide_ref[i, pl.ds(j, 8, stride=2), :] = total
    fine = relaxed(fv, fw, fa, fb, 14)
    for i in range(8):
        out_ref[i] = fine[i][0:16, 0:128] + wide_ref[i // 2]


def per_device(nx, ny, nz, right_side, coefficient):
    shape = jax.ShapeDtypeStruct
    call = functools.partial(pl.pallas_call)
    kept = [shape((8, 16, 128), F32)] * 2 + [shape((4, 8, 128), F32)] * 2 + [shape((2, 8, 128), F32)] * 2
    x_out, *own, sums = call(
        functools.partial(first_kernel, nx),
        out_shape=[shape((nx, 14, 8, 128), F32)] + kept + [shape((1, 128), F32)],
        in_specs=[VMEM] * 2,
        out_specs=[VMEM] * 8,
        scratch_shapes=[pltpu.VMEM((8, 16, 128), F32), pltpu.VMEM((4, 8, 128), F32), pltpu.VMEM((4, 8, 128), F32)],
        name="first",
    )(right_side, coefficient)
    x_in = lax.all_to_all(x_out, "gx", 0, 0, tiled=True)
    copies = jnp.broadcast_to(sums[None], (nx * ny, 1, 128))
    plane = jnp.sum(lax.all_to_all(copies, ("gx", "gy"), 0, 0, tiled=True), axis=0)
    one_out, two_out = call(
        functools.partial(second_kernel, nx, ny, nz),
        out_shape=[shape((4, 16, 8, 128), F32)] * 2,
        in_specs=[VMEM] * 7,
        out_specs=[VMEM] * 2,
        name="second",
    )(*own, x_in)
    one_in = lax.all_to_all(one_out, AXES, 0, 0, tiled=True, axis_index_groups=even_groups(nx, ny, nz))
    two_out = call(
        functools.partial(forward_kernel, ny, nz),
        out_shape=shape((4, 16, 8, 128), F32),
        in_specs=[VMEM] * 2,
        out_specs=VMEM,
        name="forward",
    )(one_in, two_out)
    two_in = lax.all_to_all(two_out, AXES, 0, 0, tiled=True, axis_index_groups=odd_groups(nx, ny, nz))
    fine, middle, coarse = (pltpu.VMEM(s, F32) for s in ((14, 24, 256), (10, 16, 128), (8, 16, 128)))
    return call(
        functools.partial(last_kernel, nx, ny, nz),
        out_shape=shape((8, 16, 128), F32),
        in_specs=[VMEM] * 10,
        out_specs=VMEM,
        scratch_shapes=[fine] * 4 + [middle] * 4 + [coarse] * 4
        + [pltpu.VMEM((4, 16, 128), F32), pltpu.VMEM((2, 8, 128), F32)],
        name="last",
    )(*own, x_in, one_in, two_in, plane)


def solution(mesh):
    nx, ny, nz = (mesh.shape[a] for a in AXES)
    spec = P(*AXES)
    return jax.shard_map(
        functools.partial(per_device, nx, ny, nz), mesh=mesh, in_specs=(spec, spec), out_specs=spec, check_vma=False
    )
```

```python
import functools
import itertools

import jax
import jax.numpy as jnp
from jax import lax
from jax.experimental import pallas as pl
from jax.experimental.pallas import tpu as pltpu
from jax.sharding import PartitionSpec as P


SWEEPS = 4
RELAX = 0.8
KEEP = 1.0 - RELAX
F32 = jnp.float32
VMEM = pl.BlockSpec(memory_space=pltpu.VMEM)
HIGHEST = lax.Precision.HIGHEST
AXES = ("gx", "gy", "gz")


def even_groups(nx, ny, nz):
    groups = []
    for gx, ya, za in itertools.product(range(nx), range(0, ny, 2), range(0, nz, 2)):
        groups.append([(gx * ny + ya + a) * nz + za + b for a in (0, 1) for b in (0, 1)])
    return groups


def odd_groups(nx, ny, nz):
    groups = []
    for gx in range(nx):
        flat = lambda gy, gz: (gx * ny + gy) * nz + gz % nz
        for ya, za in itertools.product(range(1, ny - 1, 2), range(1, nz, 2)):
            groups.append([flat(ya + a, za + b) for a in (0, 1) for b in (0, 1)])
        for gy, za in itertools.product((0, ny - 1), range(1, nz, 4)):
            groups.append([flat(gy, za + 2 * a + b) for a in (0, 1) for b in (0, 1)])
    return groups


def spots(ny, nz):
    gx, gy, gz = (lax.axis_index(a) for a in AXES)
    one = 2 * (gy & 1) + (gz & 1)
    inner = (gy > 0) & (gy < ny - 1)
    half = jnp.where(inner, (gy + 1) & 1, ((gz + nz - 1) & (nz - 1)) // 2 & 1)
    two = 2 * half + ((gz + 1) & 1)
    return gx, gy, gz, one, two, inner


def lanes(shape=(8, 128)):
    return lax.broadcasted_iota(jnp.int32, shape, len(shape) - 1)


def rows(shape=(8, 128)):
    return lax.broadcasted_iota(jnp.int32, shape, len(shape) - 2)


def turn(x, shift, axis):
    shift = shift % x.shape[axis]
    return pltpu.roll(x, shift, axis) if shift else x


def first_kernel(
    nx, ny, r_ref, c_ref, a_ref, b_ref, s_ref, v_ref, w_ref, v1_ref, w1_ref, v2_ref, w2_ref, t_ref, u_ref, d_ref,
    rv_ref, cv_ref, sems,
):
    gx = lax.axis_index("gx")
    fetches = [
        pltpu.make_async_copy(src, dst, sems.at[i]) for i, (src, dst) in enumerate(((r_ref, rv_ref), (c_ref, cv_ref)))
    ]
    for fetch in fetches:
        fetch.start()
    for fetch in fetches:
        fetch.wait()
    r, c = rv_ref[...], cv_ref[...]
    w = RELAX / (6.0 + c)
    v = w * r
    v_ref[...] = v
    w_ref[...] = w
    r4, c4 = r.reshape(4, 2, 16, 128), c.reshape(4, 2, 16, 128)
    t_ref[0:4] = r4[:, 0] + r4[:, 1]
    t_ref[4:8] = c4[:, 0] + c4[:, 1]
    a = t_ref[:, pl.ds(0, 8, stride=2), :] + t_ref[:, pl.ds(1, 8, stride=2), :]
    src, dst = rows((128, 128)), lanes((128, 128))
    half = jnp.where((src >> 1) == (dst & 63), 0.125, 0.0).astype(F32)
    one = jnp.dot(a.reshape(64, 128), half, precision=HIGHEST, preferred_element_type=F32)
    r1, c1 = one[:32].reshape(4, 8, 128), one[32:].reshape(4, 8, 128)
    d1 = RELAX / (1.5 + c1)
    v1, w1 = d1 * r1, d1 * 0.25
    v1_ref[...] = v1
    w1_ref[...] = w1
    a4 = a.reshape(4, 2, 8, 128)
    u_ref[...] = a4[:, 0] + a4[:, 1]
    e = u_ref[:, pl.ds(0, 4, stride=2), :] + u_ref[:, pl.ds(1, 4, stride=2), :]
    d_ref[:, 0:4, :] = e
    d_ref[:, 4:8, :] = e
    quarter = jnp.where((src >> 2) == (dst & 31), 0.015625, 0.0).astype(F32)
    two = jnp.dot(d_ref[...].reshape(32, 128), quarter, precision=HIGHEST, preferred_element_type=F32)
    r2, c2 = two[:16].reshape(2, 8, 128), two[16:].reshape(2, 8, 128)
    d2 = RELAX / (0.375 + c2)
    v2, w2 = d2 * r2, d2 * 0.0625
    v2_ref[...] = v2
    w2_ref[...] = w2
    lane, row = lanes(), rows()
    low = lane < 64
    sums = jnp.where(low, r2[0] + r2[1], c2[0] + c2[1])
    sums = 0.5 * jnp.sum(sums, axis=0, keepdims=True)
    quad = (lane & 63) < 32
    both = [jnp.where(quad, v2[i], w2[i]) for i in (0, 1)]
    last = jnp.where(row < 4, both[0], both[1])
    ends = [jnp.sum(jnp.where((lane >> 5) == row, v2[i], 0.0), axis=0, keepdims=True) for i in (0, 1)]
    for j in range(nx):
        far = jnp.where(j > gx, ends[1], ends[0])
        mail = jnp.concatenate([sums, far], axis=0)
        s_ref[j * ny : (j + 1) * ny] = jnp.broadcast_to(mail[None], (ny, 2, 128))
    even = (gx & 1) == 0
    for x_ref, up in ((a_ref, even), (b_ref, jnp.logical_not(even))):
        for d in range(3):
            face = jnp.where(up, v[7 - d], v[d])
            x_ref[2 * d] = face[0:8]
            x_ref[2 * d + 1] = face[8:16]
        for d in range(2):
            face = jnp.where(up, w[7 - d], w[d])
            x_ref[6 + 2 * d] = face[0:8]
            x_ref[7 + 2 * d] = face[8:16]
        for d in range(3):
            x_ref[10 + d] = jnp.where(low, jnp.where(up, v1[3 - d], v1[d]), jnp.where(up, w1[3 - d], w1[d]))
        x_ref[13] = last


def extended(gx, v_ref, w_ref, v1_ref, w1_ref, v2_ref, w2_ref, a_ref, b_ref, far=(None, None)):
    lane, row = lanes(), rows()
    low = lane < 64
    quad = (lane & 63) < 32
    even = (gx & 1) == 0
    left = lambda tile: jnp.where(even, b_ref[tile], a_ref[tile])
    right = lambda tile: jnp.where(even, a_ref[tile], b_ref[tile])

    def pair(side, tile):
        return jnp.concatenate([side(tile), side(tile + 1)], axis=0)

    def fine(side, d):
        return pair(side, 2 * d), (pair(side, 6 + 2 * d) if d < 2 else None)

    def middle(side, d):
        t = side(10 + d)
        s = turn(t, 64, 1)
        return jnp.where(low, t, s), jnp.where(low, s, t)

    def coarse(side, layer):
        t = side(13)
        s = turn(t, 4, 0)
        t = jnp.where(row < 4, t, s) if layer == 0 else jnp.where(row < 4, s, t)
        s = turn(t, 32, 1)
        return jnp.where(quad, t, s), jnp.where(quad, s, t)

    level0 = (
        [fine(left, d) for d in (2, 1, 0)]
        + [(v_ref[i], w_ref[i]) for i in range(8)]
        + [fine(right, d) for d in (0, 1, 2)]
    )
    level1 = (
        [middle(left, d) for d in (2, 1, 0)]
        + [(v1_ref[i], w1_ref[i]) for i in range(4)]
        + [middle(right, d) for d in (0, 1, 2)]
    )
    level2 = (
        [(far[0], None), coarse(left, 0), coarse(left, 1)]
        + [(v2_ref[i], w2_ref[i]) for i in range(2)]
        + [coarse(right, 0), coarse(right, 1), (far[1], None)]
    )
    return level0, level1, level2


def edge_lanes(layers):
    shape = layers[0][0].shape
    lane = lanes(shape)
    packed = jnp.zeros(shape, F32)
    for k, (v, w) in enumerate(layers):
        at = 10 * k
        packed = jnp.where((lane >= at) & (lane < at + 6), turn(v, at + 3, 1), packed)
        packed = jnp.where((lane >= at + 6) & (lane < at + 10), turn(w, at + 8, 1), packed)
    return packed


def second_kernel(ny, nz, v_ref, w_ref, v1_ref, w1_ref, v2_ref, w2_ref, a_ref, b_ref, one_ref, two_ref):
    gx, gy, _, one, two, _ = spots(ny, nz)
    level0, level1, level2 = extended(gx, v_ref, w_ref, v1_ref, w1_ref, v2_ref, w2_ref, a_ref, b_ref)
    lane, row = lanes(), rows()
    low = lane < 64
    quad = (lane & 63) < 32
    up = (gy & 1) == 0
    ends = [edge_lanes(level0[1:13])]
    ends = [ends[0][0:8], ends[0][8:16], edge_lanes(level1[1:9]), edge_lanes(level2[1:7])]
    for i, tile in enumerate(ends):
        for slot in (one ^ 1, one ^ 2, one ^ 3):
            one_ref[slot, 12 + i] = tile
        for slot in (two ^ 1, two ^ 3):
            two_ref[slot, i] = tile
    for k in range(12):
        v, w = level0[k + 1]
        if k < 8:
            a, b = level1[k + 1]
            extra = jnp.where(low, a, b)
        elif k < 11:
            a, b = (jnp.where(quad, *level2[1 + 2 * (k - 8) + i]) for i in (0, 1))
            extra = jnp.where(low, a, b)
        else:
            extra = jnp.zeros((8, 128), F32)
        high = jnp.where(row >= 5, v[8:16], jnp.where(row >= 3, turn(w[8:16], 5, 0), turn(extra, 3, 0)))
        base = jnp.where(row < 3, v[0:8], jnp.where(row < 5, turn(w[0:8], 3, 0), turn(extra, 5, 0)))
        one_ref[one ^ 2, k] = jnp.where(up, high, base)
        two_ref[two ^ 2, k] = jnp.where(up, base, high)


def forward_kernel(ny, nz, got_ref, old_ref, two_ref):
    _, _, _, one, two, _ = spots(ny, nz)
    two_ref[...] = old_ref[...]
    for i in range(4):
        two_ref[two ^ 2, 12 + i] = got_ref[one ^ 1, 12 + i]
        two_ref[two ^ 1, 12 + i] = got_ref[one ^ 2, 12 + i]


def around(v, above, below):
    return (
        above
        + below
        + turn(v, 1, 0)
        + turn(v, -1, 0)
        + turn(v, 1, 1)
        + turn(v, -1, 1)
    )


def relaxed(v_ref, w_ref, a_ref, b_ref, count):
    done = []
    for sweep in range(SWEEPS - 1):
        source = (v_ref, a_ref, b_ref)[sweep]
        target = (a_ref, b_ref, None)[sweep]
        for i in range(sweep + 1, count - sweep - 1):
            v = source[i]
            new = KEEP * v + v_ref[i] + w_ref[i] * around(v, source[i - 1], source[i + 1])
            if target is None:
                done.append(new)
            else:
                target[i] = new
    return done


def last_kernel(
    nx, ny, nz, v_ref, w_ref, v1_ref, w1_ref, v2_ref, w2_ref, ax_ref, bx_ref, one_ref, two_ref, s_ref, out_ref,
    fv, fw, fa, fb, mv, mw, ma, mb, cv, cw, ca, cb, wide_ref, deep_ref,
):
    gx, gy, gz, one, two, has_y = spots(ny, nz)
    has_z = (gz > 0) & (gz < nz - 1)
    up = (gy & 1) == 0
    ahead = (gz & 1) == 0
    lane, row = lanes(), rows()

    def far(slot, have):
        t = jnp.broadcast_to(s_ref[slot * ny + gy, 1:2], (8, 128))
        spread = jnp.zeros((8, 128), F32)
        for i in range(4):
            spread = jnp.where(row == i, turn(t, -32 * i, 1), spread)
        return jnp.where(have, spread, 0.0)

    outer_layers = far(jnp.maximum(gx - 2, 0), gx > 1), far(jnp.minimum(gx + 2, nx - 1), gx < nx - 2)
    level0, level1, level2 = extended(
        gx, v_ref, w_ref, v1_ref, w1_ref, v2_ref, w2_ref, ax_ref, bx_ref, outer_layers
    )
    part = lane - 10 * (lane // 10)
    first_half = (part < 3) | ((part >= 6) & (part < 8))
    from_one = jnp.where(ahead, jnp.where(first_half, 0, 1), jnp.where(first_half, 1, 0)) == 1

    own, plus, minus = [], [], []
    for i in range(4):
        z_two = jnp.where(has_z, two_ref[two ^ 1, i], 0.0)
        own.append(jnp.where(from_one, one_ref[one ^ 1, 12 + i], z_two))
        z_two = jnp.where(has_z, two_ref[two ^ 1, 12 + i], 0.0)
        t_one = jnp.where(from_one, one_ref[one ^ 3, 12 + i], z_two)
        z_two = jnp.where(has_z, two_ref[two ^ 3, i], 0.0)
        t_two = jnp.where(has_y, jnp.where(from_one, two_ref[two ^ 2, 12 + i], z_two), 0.0)
        plus.append(jnp.where(up, t_one, t_two))
        minus.append(jnp.where(up, t_two, t_one))
    none = jnp.zeros((8, 128), F32)

    def outer(p, m):
        return jnp.where(row < 3, p, jnp.where(row >= 5, m, none))

    z0 = jnp.concatenate([own[0], own[1], outer(plus[0], minus[1])], axis=0)
    z1 = jnp.concatenate([own[2], outer(plus[2], minus[2])], axis=0)
    z2 = jnp.concatenate([jnp.where(row < 4, own[3], plus[3]), jnp.where(row >= 5, minus[3], none)], axis=0)

    lane16 = lanes((16, 128))
    fv[0, 0:16, 0:128] = level0[0][0]
    fv[13, 0:16, 0:128] = level0[13][0]
    for i in (0, 13):
        fv[i, 16:24, 0:128] = none
        fv[i, :, 128:256] = jnp.zeros((24, 128), F32)
    for k in range(12):
        a = one_ref[one ^ 2, k]
        b = jnp.where(has_y, two_ref[two ^ 2, k], 0.0)
        p, m = jnp.where(up, a, b), jnp.where(up, b, a)
        v, w = level0[k + 1]
        fv[k + 1, 0:16, 0:128] = v
        fw[k + 1, 0:16, 0:128] = w
        fv[k + 1, 16:24, 0:128] = outer(p, m)
        fw[k + 1, 16:24, 0:128] = jnp.where(row < 2, turn(p, 5, 0), jnp.where(row >= 6, turn(m, 3, 0), none))
        fv[k + 1, :, 128:256] = turn(z0, -(10 * k + 3), 1)
        fw[k + 1, :, 128:256] = turn(z0, -(10 * k + 8), 1)
        if k < 8:
            extra = outer(turn(p, 3, 0), turn(m, 5, 0))
            v, w = level1[k + 1]
            v = jnp.concatenate([v, extra], axis=0)
            w = jnp.concatenate([w, turn(extra, 64, 1)], axis=0)
            at = 10 * k + 3
            mv[k + 1] = jnp.where(lane16 < 64, v, jnp.where(lane16 < 96, turn(z1, 64 - at, 1), turn(z1, -at, 1)))
            at = 10 * k + 8
            mw[k + 1] = jnp.where(lane16 < 64, w, jnp.where(lane16 < 96, turn(z1, 64 - at, 1), turn(z1, -at, 1)))
        elif k < 11:
            near, far = turn(p, 7, 0), turn(m, 5, 0)
            for i in (0, 1):
                j = 2 * (k - 8) + i
                v, w = level2[j + 1]
                for field, target in ((0, cv), (1, cw)):
                    shift = -(64 * i + 32 * field)
                    top = jnp.where(row < 4, (v, w)[field], turn(near, shift, 1))
                    full = jnp.concatenate([top, jnp.where(row >= 5, turn(far, shift, 1), none)], axis=0)
                    at = 10 * j + (3, 8)[field]
                    ends = jnp.where(lane16 < 64, turn(z2, 32 - at, 1), turn(z2, -at, 1))
                    target[j + 1] = jnp.where(lane16 < 32, full, ends)
    for i in (0, 9):
        mv[i, 0:8] = level1[i][0]
        mv[i, 8:16] = none
    for i in (0, 7):
        cv[i, 0:8] = level2[i][0]
        cv[i, 8:16] = none

    coarse = relaxed(cv, cw, ca, cb, 8)
    s = jnp.sum(s_ref[...], axis=0)[0:1]
    plane = jnp.where(lane < 64, s / (turn(jnp.broadcast_to(s, (8, 128)), 64, 1) + 16.0), 0.0)
    src, dst = rows((128, 128)), lanes((128, 128))
    spread4 = jnp.where(src == (dst >> 2), 1.0, 0.0).astype(F32)
    spread2 = jnp.where(src == (dst >> 1), 1.0, 0.0).astype(F32)
    c = jnp.concatenate([layer[0:8] + plane for layer in coarse], axis=0)
    c = jnp.dot(c, spread4, precision=HIGHEST, preferred_element_type=F32).reshape(2, 8, 128)
    middle = relaxed(mv, mw, ma, mb, 10)
    m = jnp.concatenate([layer[0:8] for layer in middle], axis=0)
    m = jnp.dot(m, spread2, precision=HIGHEST, preferred_element_type=F32).reshape(4, 8, 128)
    for i in range(2):
        for j in range(2):
            deep_ref[i, pl.ds(j, 4, stride=2), :] = c[i, 0:4]
    for i in range(4):
        total = m[i] + deep_ref[i // 2]
        for j in range(2):
            wide_ref[i, pl.ds(j, 8, stride=2), :] = total
    fine = relaxed(fv, fw, fa, fb, 14)
    for i in range(8):
        out_ref[i] = fine[i][0:16, 0:128] + wide_ref[i // 2]


def per_device(nx, ny, nz, right_side, coefficient):
    shape = jax.ShapeDtypeStruct
    call = pl.pallas_call
    kept = [shape((8, 16, 128), F32)] * 2 + [shape((4, 8, 128), F32)] * 2 + [shape((2, 8, 128), F32)] * 2
    a_out, b_out, s_out, *own = call(
        functools.partial(first_kernel, nx, ny),
        out_shape=[shape((14, 8, 128), F32)] * 2 + [shape((nx * ny, 2, 128), F32)] + kept,
        in_specs=[pl.BlockSpec(memory_space=pltpu.HBM)] * 2,
        out_specs=[VMEM] * 9,
        scratch_shapes=[pltpu.VMEM(s, F32) for s in ((8, 16, 128), (4, 8, 128), (4, 8, 128), (8, 16, 128), (8, 16, 128))]
        + [pltpu.SemaphoreType.DMA((2,))],
        compiler_params=pltpu.CompilerParams(vmem_limit_bytes=8 << 20),
        name="first",
    )(right_side, coefficient)
    near = [(i, i ^ 1) for i in range(nx)]
    across = [(i, i + 1 if i & 1 else i - 1) for i in range(1, nx - 1)]
    b_in = lax.ppermute(b_out, "gx", across)
    s_in = lax.all_to_all(s_out, ("gx", "gy"), 0, 0, tiled=True)
    a_in = lax.ppermute(a_out, "gx", near)
    one_out, two_out = call(
        functools.partial(second_kernel, ny, nz),
        out_shape=[shape((4, 16, 8, 128), F32)] * 2,
        in_specs=[VMEM] * 8,
        out_specs=[VMEM] * 2,
        compiler_params=pltpu.CompilerParams(vmem_limit_bytes=8 << 20),
        name="second",
    )(*own, a_in, b_in)
    one_out, s_in = lax.optimization_barrier((one_out, s_in))
    one_in = lax.all_to_all(one_out, AXES, 0, 0, tiled=True, axis_index_groups=even_groups(nx, ny, nz))
    two_out = call(
        functools.partial(forward_kernel, ny, nz),
        out_shape=shape((4, 16, 8, 128), F32),
        in_specs=[VMEM] * 2,
        out_specs=VMEM,
        compiler_params=pltpu.CompilerParams(vmem_limit_bytes=8 << 20),
        name="forward",
    )(one_in, two_out)
    two_in = lax.all_to_all(two_out, AXES, 0, 0, tiled=True, axis_index_groups=odd_groups(nx, ny, nz))
    fine, middle, coarse = (pltpu.VMEM(s, F32) for s in ((14, 24, 256), (10, 16, 128), (8, 16, 128)))
    return call(
        functools.partial(last_kernel, nx, ny, nz),
        out_shape=shape((8, 16, 128), F32),
        in_specs=[VMEM] * 11,
        out_specs=VMEM,
        scratch_shapes=[fine] * 4 + [middle] * 4 + [coarse] * 4
        + [pltpu.VMEM((4, 16, 128), F32), pltpu.VMEM((2, 8, 128), F32)],
        compiler_params=pltpu.CompilerParams(vmem_limit_bytes=8 << 20),
        name="last",
    )(*own, a_in, b_in, one_in, two_in, s_in)


def solution(mesh):
    nx, ny, nz = (mesh.shape[a] for a in AXES)
    spec = P(*AXES)
    body = functools.partial(per_device, nx, ny, nz)

    return jax.shard_map(body, mesh=mesh, in_specs=(spec, spec), out_specs=spec, check_vma=False)
```

```python
import functools

import jax
import jax.numpy as jnp
from jax import lax
from jax.experimental import pallas as pl
from jax.experimental.pallas import tpu as pltpu
from jax.sharding import PartitionSpec as P


SWEEPS = 4
RELAX = 0.8
KEEP = 1.0 - RELAX
F32 = jnp.float32
VMEM = pl.BlockSpec(memory_space=pltpu.VMEM)
HIGHEST = lax.Precision.HIGHEST
AXES = ("gx", "gy", "gz")


def lanes(shape=(8, 128)):
    return lax.broadcasted_iota(jnp.int32, shape, len(shape) - 1)


def rows(shape=(8, 128)):
    return lax.broadcasted_iota(jnp.int32, shape, len(shape) - 2)


def turn(x, shift, axis):
    shift = shift % x.shape[axis]
    return pltpu.roll(x, shift, axis) if shift else x


def first_kernel(
    nx, ny, r_ref, c_ref, a_ref, b_ref, s_ref, v_ref, w_ref, v1_ref, w1_ref, v2_ref, w2_ref, t_ref, u_ref, d_ref,
    rv_ref, cv_ref, sems,
):
    gx = lax.axis_index("gx")
    fetches = [
        pltpu.make_async_copy(src, dst, sems.at[i]) for i, (src, dst) in enumerate(((r_ref, rv_ref), (c_ref, cv_ref)))
    ]
    for fetch in fetches:
        fetch.start()
    for fetch in fetches:
        fetch.wait()
    r, c = rv_ref[...], cv_ref[...]
    w = RELAX / (6.0 + c)
    v = w * r
    v_ref[...] = v
    w_ref[...] = w
    r4, c4 = r.reshape(4, 2, 16, 128), c.reshape(4, 2, 16, 128)
    t_ref[0:4] = r4[:, 0] + r4[:, 1]
    t_ref[4:8] = c4[:, 0] + c4[:, 1]
    a = t_ref[:, pl.ds(0, 8, stride=2), :] + t_ref[:, pl.ds(1, 8, stride=2), :]
    src, dst = rows((128, 128)), lanes((128, 128))
    half = jnp.where((src >> 1) == (dst & 63), 0.125, 0.0).astype(F32)
    one = jnp.dot(a.reshape(64, 128), half, precision=HIGHEST, preferred_element_type=F32)
    r1, c1 = one[:32].reshape(4, 8, 128), one[32:].reshape(4, 8, 128)
    d1 = RELAX / (1.5 + c1)
    v1, w1 = d1 * r1, d1 * 0.25
    v1_ref[...] = v1
    w1_ref[...] = w1
    a4 = a.reshape(4, 2, 8, 128)
    u_ref[...] = a4[:, 0] + a4[:, 1]
    e = u_ref[:, pl.ds(0, 4, stride=2), :] + u_ref[:, pl.ds(1, 4, stride=2), :]
    d_ref[:, 0:4, :] = e
    d_ref[:, 4:8, :] = e
    quarter = jnp.where((src >> 2) == (dst & 31), 0.015625, 0.0).astype(F32)
    two = jnp.dot(d_ref[...].reshape(32, 128), quarter, precision=HIGHEST, preferred_element_type=F32)
    r2, c2 = two[:16].reshape(2, 8, 128), two[16:].reshape(2, 8, 128)
    d2 = RELAX / (0.375 + c2)
    v2, w2 = d2 * r2, d2 * 0.0625
    v2_ref[...] = v2
    w2_ref[...] = w2
    lane, row = lanes(), rows()
    low = lane < 64
    sums = jnp.where(low, r2[0] + r2[1], c2[0] + c2[1])
    sums = 0.5 * jnp.sum(sums, axis=0, keepdims=True)
    quad = (lane & 63) < 32
    both = [jnp.where(quad, v2[i], w2[i]) for i in (0, 1)]
    last = jnp.where(row < 4, both[0], both[1])
    ends = [jnp.sum(jnp.where((lane >> 5) == row, v2[i], 0.0), axis=0, keepdims=True) for i in (0, 1)]
    for j in range(nx):
        far = jnp.where(j > gx, ends[1], ends[0])
        mail = jnp.concatenate([sums, far], axis=0)
        s_ref[j * ny : (j + 1) * ny] = jnp.broadcast_to(mail[None], (ny, 2, 128))
    even = (gx & 1) == 0
    for x_ref, up in ((a_ref, even), (b_ref, jnp.logical_not(even))):
        for d in range(3):
            face = jnp.where(up, v[7 - d], v[d])
            x_ref[2 * d] = face[0:8]
            x_ref[2 * d + 1] = face[8:16]
        for d in range(2):
            face = jnp.where(up, w[7 - d], w[d])
            x_ref[6 + 2 * d] = face[0:8]
            x_ref[7 + 2 * d] = face[8:16]
        for d in range(3):
            x_ref[10 + d] = jnp.where(low, jnp.where(up, v1[3 - d], v1[d]), jnp.where(up, w1[3 - d], w1[d]))
        x_ref[13] = last


def extended(gx, v_ref, w_ref, v1_ref, w1_ref, v2_ref, w2_ref, a_ref, b_ref, far=(None, None)):
    lane, row = lanes(), rows()
    low = lane < 64
    quad = (lane & 63) < 32
    even = (gx & 1) == 0
    left = lambda tile: jnp.where(even, b_ref[tile], a_ref[tile])
    right = lambda tile: jnp.where(even, a_ref[tile], b_ref[tile])

    def pair(side, tile):
        return jnp.concatenate([side(tile), side(tile + 1)], axis=0)

    def fine(side, d):
        return pair(side, 2 * d), (pair(side, 6 + 2 * d) if d < 2 else None)

    def middle(side, d):
        t = side(10 + d)
        s = turn(t, 64, 1)
        return jnp.where(low, t, s), jnp.where(low, s, t)

    def coarse(side, layer):
        t = side(13)
        s = turn(t, 4, 0)
        t = jnp.where(row < 4, t, s) if layer == 0 else jnp.where(row < 4, s, t)
        s = turn(t, 32, 1)
        return jnp.where(quad, t, s), jnp.where(quad, s, t)

    level0 = (
        [fine(left, d) for d in (2, 1, 0)]
        + [(v_ref[i], w_ref[i]) for i in range(8)]
        + [fine(right, d) for d in (0, 1, 2)]
    )
    level1 = (
        [middle(left, d) for d in (2, 1, 0)]
        + [(v1_ref[i], w1_ref[i]) for i in range(4)]
        + [middle(right, d) for d in (0, 1, 2)]
    )
    level2 = (
        [(far[0], None), coarse(left, 0), coarse(left, 1)]
        + [(v2_ref[i], w2_ref[i]) for i in range(2)]
        + [coarse(right, 0), coarse(right, 1), (far[1], None)]
    )
    return level0, level1, level2


def edge_lanes(layers):
    shape = layers[0][0].shape
    lane = lanes(shape)
    packed = jnp.zeros(shape, F32)
    for k, (v, w) in enumerate(layers):
        at = 10 * k
        packed = jnp.where((lane >= at) & (lane < at + 6), turn(v, at + 3, 1), packed)
        packed = jnp.where((lane >= at + 6) & (lane < at + 10), turn(w, at + 8, 1), packed)
    return packed


def second_kernel(v_ref, w_ref, v1_ref, w1_ref, v2_ref, w2_ref, a_ref, b_ref, z_ref, ya_ref, yb_ref):
    gx, gy = lax.axis_index("gx"), lax.axis_index("gy")
    level0, level1, level2 = extended(gx, v_ref, w_ref, v1_ref, w1_ref, v2_ref, w2_ref, a_ref, b_ref)
    lane, row = lanes(), rows()
    low = lane < 64
    quad = (lane & 63) < 32
    up = (gy & 1) == 0
    ends = edge_lanes(level0[1:13])
    for i, tile in enumerate((ends[0:8], ends[8:16], edge_lanes(level1[1:9]), edge_lanes(level2[1:7]))):
        z_ref[i] = tile
    for k in range(12):
        v, w = level0[k + 1]
        if k < 8:
            a, b = level1[k + 1]
            extra = jnp.where(low, a, b)
        elif k < 11:
            a, b = (jnp.where(quad, *level2[1 + 2 * (k - 8) + i]) for i in (0, 1))
            extra = jnp.where(low, a, b)
        else:
            extra = jnp.zeros((8, 128), F32)
        high = jnp.where(row >= 5, v[8:16], jnp.where(row >= 3, turn(w[8:16], 5, 0), turn(extra, 3, 0)))
        base = jnp.where(row < 3, v[0:8], jnp.where(row < 5, turn(w[0:8], 3, 0), turn(extra, 5, 0)))
        ya_ref[k] = jnp.where(up, high, base)
        yb_ref[k] = jnp.where(up, base, high)


def both_ends(i, za_ref, zb_ref):
    lane = lanes()
    part = lane - 10 * (lane // 10)
    ahead = (lax.axis_index("gz") & 1) == 0
    last = (part < 3) | ((part >= 6) & (part < 8))
    from_a = jnp.where(ahead, jnp.where(last, 0, 1), jnp.where(last, 1, 0)) == 1
    return jnp.where(from_a, za_ref[i], zb_ref[i])


def third_kernel(za_ref, zb_ref, ya_ref, yb_ref, ya_out, yb_out):
    ya_out[0:12] = ya_ref[...]
    yb_out[0:12] = yb_ref[...]
    for i in range(4):
        ends = both_ends(i, za_ref, zb_ref)
        ya_out[12 + i] = ends
        yb_out[12 + i] = ends


def around(v, above, below):
    return (
        above
        + below
        + turn(v, 1, 0)
        + turn(v, -1, 0)
        + turn(v, 1, 1)
        + turn(v, -1, 1)
    )


def relaxed(v_ref, w_ref, a_ref, b_ref, count):
    done = []
    for sweep in range(SWEEPS - 1):
        source = (v_ref, a_ref, b_ref)[sweep]
        target = (a_ref, b_ref, None)[sweep]
        for i in range(sweep + 1, count - sweep - 1):
            v = source[i]
            new = KEEP * v + v_ref[i] + w_ref[i] * around(v, source[i - 1], source[i + 1])
            if target is None:
                done.append(new)
            else:
                target[i] = new
    return done


def last_kernel(
    nx, ny, v_ref, w_ref, v1_ref, w1_ref, v2_ref, w2_ref, ax_ref, bx_ref, za_ref, zb_ref, ya_ref, yb_ref, s_ref, out_ref,
    fv, fw, fa, fb, mv, mw, ma, mb, cv, cw, ca, cb, wide_ref, deep_ref,
):
    gx, gy = lax.axis_index("gx"), lax.axis_index("gy")
    up = (gy & 1) == 0
    lane, row = lanes(), rows()

    def far(slot, have):
        t = jnp.broadcast_to(s_ref[slot * ny + gy, 1:2], (8, 128))
        spread = jnp.zeros((8, 128), F32)
        for i in range(4):
            spread = jnp.where(row == i, turn(t, -32 * i, 1), spread)
        return jnp.where(have, spread, 0.0)

    outer_layers = far(jnp.maximum(gx - 2, 0), gx > 1), far(jnp.minimum(gx + 2, nx - 1), gx < nx - 2)
    level0, level1, level2 = extended(
        gx, v_ref, w_ref, v1_ref, w1_ref, v2_ref, w2_ref, ax_ref, bx_ref, outer_layers
    )

    def sides(k):
        a, b = ya_ref[k], yb_ref[k]
        return jnp.where(up, a, b), jnp.where(up, b, a)

    own = [both_ends(i, za_ref, zb_ref) for i in range(4)]
    plus, minus = zip(*(sides(12 + i) for i in range(4)))
    none = jnp.zeros((8, 128), F32)

    def outer(p, m):
        return jnp.where(row < 3, p, jnp.where(row >= 5, m, none))

    z0 = jnp.concatenate([own[0], own[1], outer(plus[0], minus[1])], axis=0)
    z1 = jnp.concatenate([own[2], outer(plus[2], minus[2])], axis=0)
    z2 = jnp.concatenate([jnp.where(row < 4, own[3], plus[3]), jnp.where(row >= 5, minus[3], none)], axis=0)

    lane16 = lanes((16, 128))
    fv[0, 0:16, 0:128] = level0[0][0]
    fv[13, 0:16, 0:128] = level0[13][0]
    for i in (0, 13):
        fv[i, 16:24, 0:128] = none
        fv[i, :, 128:256] = jnp.zeros((24, 128), F32)
    for k in range(12):
        p, m = sides(k)
        v, w = level0[k + 1]
        fv[k + 1, 0:16, 0:128] = v
        fw[k + 1, 0:16, 0:128] = w
        fv[k + 1, 16:24, 0:128] = outer(p, m)
        fw[k + 1, 16:24, 0:128] = jnp.where(row < 2, turn(p, 5, 0), jnp.where(row >= 6, turn(m, 3, 0), none))
        fv[k + 1, :, 128:256] = turn(z0, -(10 * k + 3), 1)
        fw[k + 1, :, 128:256] = turn(z0, -(10 * k + 8), 1)
        if k < 8:
            extra = outer(turn(p, 3, 0), turn(m, 5, 0))
            v, w = level1[k + 1]
            v = jnp.concatenate([v, extra], axis=0)
            w = jnp.concatenate([w, turn(extra, 64, 1)], axis=0)
            at = 10 * k + 3
            mv[k + 1] = jnp.where(lane16 < 64, v, jnp.where(lane16 < 96, turn(z1, 64 - at, 1), turn(z1, -at, 1)))
            at = 10 * k + 8
            mw[k + 1] = jnp.where(lane16 < 64, w, jnp.where(lane16 < 96, turn(z1, 64 - at, 1), turn(z1, -at, 1)))
        elif k < 11:
            near, far = turn(p, 7, 0), turn(m, 5, 0)
            for i in (0, 1):
                j = 2 * (k - 8) + i
                v, w = level2[j + 1]
                for field, target in ((0, cv), (1, cw)):
                    shift = -(64 * i + 32 * field)
                    top = jnp.where(row < 4, (v, w)[field], turn(near, shift, 1))
                    full = jnp.concatenate([top, jnp.where(row >= 5, turn(far, shift, 1), none)], axis=0)
                    at = 10 * j + (3, 8)[field]
                    ends = jnp.where(lane16 < 64, turn(z2, 32 - at, 1), turn(z2, -at, 1))
                    target[j + 1] = jnp.where(lane16 < 32, full, ends)
    for i in (0, 9):
        mv[i, 0:8] = level1[i][0]
        mv[i, 8:16] = none
    for i in (0, 7):
        cv[i, 0:8] = level2[i][0]
        cv[i, 8:16] = none

    coarse = relaxed(cv, cw, ca, cb, 8)
    s = jnp.sum(s_ref[...], axis=0)[0:1]
    plane = jnp.where(lane < 64, s / (turn(jnp.broadcast_to(s, (8, 128)), 64, 1) + 16.0), 0.0)
    src, dst = rows((128, 128)), lanes((128, 128))
    spread4 = jnp.where(src == (dst >> 2), 1.0, 0.0).astype(F32)
    spread2 = jnp.where(src == (dst >> 1), 1.0, 0.0).astype(F32)
    c = jnp.concatenate([layer[0:8] + plane for layer in coarse], axis=0)
    c = jnp.dot(c, spread4, precision=HIGHEST, preferred_element_type=F32).reshape(2, 8, 128)
    middle = relaxed(mv, mw, ma, mb, 10)
    m = jnp.concatenate([layer[0:8] for layer in middle], axis=0)
    m = jnp.dot(m, spread2, precision=HIGHEST, preferred_element_type=F32).reshape(4, 8, 128)
    for i in range(2):
        for j in range(2):
            deep_ref[i, pl.ds(j, 4, stride=2), :] = c[i, 0:4]
    for i in range(4):
        total = m[i] + deep_ref[i // 2]
        for j in range(2):
            wide_ref[i, pl.ds(j, 8, stride=2), :] = total
    fine = relaxed(fv, fw, fa, fb, 14)
    for i in range(8):
        out_ref[i] = fine[i][0:16, 0:128] + wide_ref[i // 2]


def per_device(nx, ny, nz, right_side, coefficient):
    shape = jax.ShapeDtypeStruct
    call = pl.pallas_call
    kept = [shape((8, 16, 128), F32)] * 2 + [shape((4, 8, 128), F32)] * 2 + [shape((2, 8, 128), F32)] * 2
    a_out, b_out, s_out, *own = call(
        functools.partial(first_kernel, nx, ny),
        out_shape=[shape((14, 8, 128), F32)] * 2 + [shape((nx * ny, 2, 128), F32)] + kept,
        in_specs=[pl.BlockSpec(memory_space=pltpu.HBM)] * 2,
        out_specs=[VMEM] * 9,
        scratch_shapes=[pltpu.VMEM(s, F32) for s in ((8, 16, 128), (4, 8, 128), (4, 8, 128), (8, 16, 128), (8, 16, 128))]
        + [pltpu.SemaphoreType.DMA((2,))],
        compiler_params=pltpu.CompilerParams(vmem_limit_bytes=8 << 20),
        name="first",
    )(right_side, coefficient)
    even = lambda n: [(i, i ^ 1) for i in range(n)]
    odd = lambda n: [(i, i + 1 if i & 1 else i - 1) for i in range(1, n - 1)]
    b_in = lax.ppermute(b_out, "gx", odd(nx))
    s_in = lax.all_to_all(s_out, ("gx", "gy"), 0, 0, tiled=True)
    a_in = lax.ppermute(a_out, "gx", even(nx))
    limit = pltpu.CompilerParams(vmem_limit_bytes=8 << 20)
    z_out, ya_own, yb_own = call(
        second_kernel,
        out_shape=[shape((4, 8, 128), F32)] + [shape((12, 8, 128), F32)] * 2,
        in_specs=[VMEM] * 8,
        out_specs=[VMEM] * 3,
        compiler_params=limit,
        name="second",
    )(*own, a_in, b_in)
    zb_in = lax.ppermute(z_out, "gz", odd(nz))
    za_in = lax.ppermute(z_out, "gz", even(nz))
    ya_out, yb_out = call(
        third_kernel,
        out_shape=[shape((16, 8, 128), F32)] * 2,
        in_specs=[VMEM] * 4,
        out_specs=[VMEM] * 2,
        compiler_params=limit,
        name="third",
    )(za_in, zb_in, ya_own, yb_own)
    yb_in = lax.ppermute(yb_out, "gy", odd(ny))
    ya_in = lax.ppermute(ya_out, "gy", even(ny))
    fine, middle, coarse = (pltpu.VMEM(s, F32) for s in ((14, 24, 256), (10, 16, 128), (8, 16, 128)))
    return call(
        functools.partial(last_kernel, nx, ny),
        out_shape=shape((8, 16, 128), F32),
        in_specs=[VMEM] * 13,
        out_specs=VMEM,
        scratch_shapes=[fine] * 4 + [middle] * 4 + [coarse] * 4
        + [pltpu.VMEM((4, 16, 128), F32), pltpu.VMEM((2, 8, 128), F32)],
        compiler_params=pltpu.CompilerParams(vmem_limit_bytes=8 << 20),
        name="last",
    )(*own, a_in, b_in, za_in, zb_in, ya_in, yb_in, s_in)


def solution(mesh):
    nx, ny, nz = (mesh.shape[a] for a in AXES)
    spec = P(*AXES)
    body = functools.partial(per_device, nx, ny, nz)

    return jax.shard_map(body, mesh=mesh, in_specs=(spec, spec), out_specs=spec, check_vma=False)
```

```python
import functools

import jax
import jax.numpy as jnp
from jax import lax
from jax.experimental import pallas as pl
from jax.experimental.pallas import tpu as pltpu
from jax.sharding import PartitionSpec as P


SWEEPS = 4
RELAX = 0.8
KEEP = 1.0 - RELAX
F32 = jnp.float32
VMEM = pl.BlockSpec(memory_space=pltpu.VMEM)
HIGHEST = lax.Precision.HIGHEST
AXES = ("gx", "gy", "gz")


def lanes(shape=(8, 128)):
    return lax.broadcasted_iota(jnp.int32, shape, len(shape) - 1)


def rows(shape=(8, 128)):
    return lax.broadcasted_iota(jnp.int32, shape, len(shape) - 2)


def turn(x, shift, axis):
    shift = shift % x.shape[axis]
    return pltpu.roll(x, shift, axis) if shift else x


def first_kernel(
    nx, ny, in_ref, a_ref, b_ref, s_ref, v_ref, w_ref, v1_ref, w1_ref, v2_ref, w2_ref, t_ref, u_ref, d_ref,
):
    gx = lax.axis_index("gx")
    r, c = in_ref[0], in_ref[1]
    w = RELAX / (6.0 + c)
    v = w * r
    v_ref[...] = v
    w_ref[...] = w
    r4, c4 = r.reshape(4, 2, 16, 128), c.reshape(4, 2, 16, 128)
    t_ref[0:4] = r4[:, 0] + r4[:, 1]
    t_ref[4:8] = c4[:, 0] + c4[:, 1]
    a = t_ref[:, pl.ds(0, 8, stride=2), :] + t_ref[:, pl.ds(1, 8, stride=2), :]
    src, dst = rows((128, 128)), lanes((128, 128))
    half = jnp.where((src >> 1) == (dst & 63), 0.125, 0.0).astype(F32)
    one = jnp.dot(a.reshape(64, 128), half, precision=HIGHEST, preferred_element_type=F32)
    r1, c1 = one[:32].reshape(4, 8, 128), one[32:].reshape(4, 8, 128)
    d1 = RELAX / (1.5 + c1)
    v1, w1 = d1 * r1, d1 * 0.25
    v1_ref[...] = v1
    w1_ref[...] = w1
    a4 = a.reshape(4, 2, 8, 128)
    u_ref[...] = a4[:, 0] + a4[:, 1]
    e = u_ref[:, pl.ds(0, 4, stride=2), :] + u_ref[:, pl.ds(1, 4, stride=2), :]
    d_ref[:, 0:4, :] = e
    d_ref[:, 4:8, :] = e
    quarter = jnp.where((src >> 2) == (dst & 31), 0.015625, 0.0).astype(F32)
    two = jnp.dot(d_ref[...].reshape(32, 128), quarter, precision=HIGHEST, preferred_element_type=F32)
    r2, c2 = two[:16].reshape(2, 8, 128), two[16:].reshape(2, 8, 128)
    d2 = RELAX / (0.375 + c2)
    v2, w2 = d2 * r2, d2 * 0.0625
    v2_ref[...] = v2
    w2_ref[...] = w2
    lane, row = lanes(), rows()
    low = lane < 64
    sums = jnp.where(low, r2[0] + r2[1], c2[0] + c2[1])
    sums = 0.5 * jnp.sum(sums, axis=0, keepdims=True)
    quad = (lane & 63) < 32
    both = [jnp.where(quad, v2[i], w2[i]) for i in (0, 1)]
    last = jnp.where(row < 4, both[0], both[1])
    ends = [jnp.sum(jnp.where((lane >> 5) == row, v2[i], 0.0), axis=0, keepdims=True) for i in (0, 1)]
    for j in range(nx):
        far = jnp.where(j > gx, ends[1], ends[0])
        mail = jnp.concatenate([sums, far], axis=0)
        s_ref[j * ny : (j + 1) * ny] = jnp.broadcast_to(mail[None], (ny, 2, 128))
    even = (gx & 1) == 0
    for x_ref, up in ((a_ref, even), (b_ref, jnp.logical_not(even))):
        for d in range(3):
            face = jnp.where(up, v[7 - d], v[d])
            x_ref[2 * d] = face[0:8]
            x_ref[2 * d + 1] = face[8:16]
        for d in range(2):
            face = jnp.where(up, w[7 - d], w[d])
            x_ref[6 + 2 * d] = face[0:8]
            x_ref[7 + 2 * d] = face[8:16]
        for d in range(3):
            x_ref[10 + d] = jnp.where(low, jnp.where(up, v1[3 - d], v1[d]), jnp.where(up, w1[3 - d], w1[d]))
        x_ref[13] = last


def extended(gx, v_ref, w_ref, v1_ref, w1_ref, v2_ref, w2_ref, al_ref, ah_ref, b_ref, far=(None, None)):
    lane, row = lanes(), rows()
    low = lane < 64
    quad = (lane & 63) < 32
    even = (gx & 1) == 0
    near = lambda tile: al_ref[tile] + ah_ref[tile]
    left = lambda tile: jnp.where(even, b_ref[tile], near(tile))
    right = lambda tile: jnp.where(even, near(tile), b_ref[tile])

    def pair(side, tile):
        return jnp.concatenate([side(tile), side(tile + 1)], axis=0)

    def fine(side, d):
        return pair(side, 2 * d), (pair(side, 6 + 2 * d) if d < 2 else None)

    def middle(side, d):
        t = side(10 + d)
        s = turn(t, 64, 1)
        return jnp.where(low, t, s), jnp.where(low, s, t)

    def coarse(side, layer):
        t = side(13)
        s = turn(t, 4, 0)
        t = jnp.where(row < 4, t, s) if layer == 0 else jnp.where(row < 4, s, t)
        s = turn(t, 32, 1)
        return jnp.where(quad, t, s), jnp.where(quad, s, t)

    level0 = (
        [fine(left, d) for d in (2, 1, 0)]
        + [(v_ref[i], w_ref[i]) for i in range(8)]
        + [fine(right, d) for d in (0, 1, 2)]
    )
    level1 = (
        [middle(left, d) for d in (2, 1, 0)]
        + [(v1_ref[i], w1_ref[i]) for i in range(4)]
        + [middle(right, d) for d in (0, 1, 2)]
    )
    level2 = (
        [(far[0], None), coarse(left, 0), coarse(left, 1)]
        + [(v2_ref[i], w2_ref[i]) for i in range(2)]
        + [coarse(right, 0), coarse(right, 1), (far[1], None)]
    )
    return level0, level1, level2


def edge_lanes(layers):
    shape = layers[0][0].shape
    lane = lanes(shape)
    packed = jnp.zeros(shape, F32)
    for k, (v, w) in enumerate(layers):
        at = 10 * k
        packed = jnp.where((lane >= at) & (lane < at + 6), turn(v, at + 3, 1), packed)
        packed = jnp.where((lane >= at + 6) & (lane < at + 10), turn(w, at + 8, 1), packed)
    return packed


def second_kernel(v_ref, w_ref, v1_ref, w1_ref, v2_ref, w2_ref, al_ref, ah_ref, b_ref, z_ref, ya_ref, yb_ref):
    gx, gy = lax.axis_index("gx"), lax.axis_index("gy")
    level0, level1, level2 = extended(gx, v_ref, w_ref, v1_ref, w1_ref, v2_ref, w2_ref, al_ref, ah_ref, b_ref)
    lane, row = lanes(), rows()
    low = lane < 64
    quad = (lane & 63) < 32
    up = (gy & 1) == 0
    ends = edge_lanes(level0[1:13])
    for i, tile in enumerate((ends[0:8], ends[8:16], edge_lanes(level1[1:9]), edge_lanes(level2[1:7]))):
        z_ref[i] = tile
    for k in range(12):
        v, w = level0[k + 1]
        if k < 8:
            a, b = level1[k + 1]
            extra = jnp.where(low, a, b)
        elif k < 11:
            a, b = (jnp.where(quad, *level2[1 + 2 * (k - 8) + i]) for i in (0, 1))
            extra = jnp.where(low, a, b)
        else:
            extra = jnp.zeros((8, 128), F32)
        high = jnp.where(row >= 5, v[8:16], jnp.where(row >= 3, turn(w[8:16], 5, 0), turn(extra, 3, 0)))
        base = jnp.where(row < 3, v[0:8], jnp.where(row < 5, turn(w[0:8], 3, 0), turn(extra, 5, 0)))
        ya_ref[k] = jnp.where(up, high, base)
        yb_ref[k] = jnp.where(up, base, high)


def both_ends(i, za_ref, zb_ref):
    lane = lanes()
    part = lane - 10 * (lane // 10)
    ahead = (lax.axis_index("gz") & 1) == 0
    last = (part < 3) | ((part >= 6) & (part < 8))
    from_a = jnp.where(ahead, jnp.where(last, 0, 1), jnp.where(last, 1, 0)) == 1
    return jnp.where(from_a, za_ref[i], zb_ref[i])


def third_kernel(za_ref, zb_ref, ya_ref, yb_ref, ya_out, yb_out):
    ya_out[0:12] = ya_ref[...]
    yb_out[0:12] = yb_ref[...]
    for i in range(4):
        ends = both_ends(i, za_ref, zb_ref)
        ya_out[12 + i] = ends
        yb_out[12 + i] = ends


def around(v, above, below):
    return (
        above
        + below
        + turn(v, 1, 0)
        + turn(v, -1, 0)
        + turn(v, 1, 1)
        + turn(v, -1, 1)
    )


def relaxed(v_ref, w_ref, a_ref, b_ref, count):
    done = []
    for sweep in range(SWEEPS - 1):
        source = (v_ref, a_ref, b_ref)[sweep]
        target = (a_ref, b_ref, None)[sweep]
        for i in range(sweep + 1, count - sweep - 1):
            v = source[i]
            new = KEEP * v + v_ref[i] + w_ref[i] * around(v, source[i - 1], source[i + 1])
            if target is None:
                done.append(new)
            else:
                target[i] = new
    return done


def last_kernel(
    nx, ny, v_ref, w_ref, v1_ref, w1_ref, v2_ref, w2_ref, al_ref, ah_ref, b_ref, za_ref, zb_ref, ya_ref, yb_ref, s_ref, out_ref,
    fv, fw, fa, fb, mv, mw, ma, mb, cv, cw, ca, cb, wide_ref, deep_ref,
):
    gx, gy = lax.axis_index("gx"), lax.axis_index("gy")
    up = (gy & 1) == 0
    lane, row = lanes(), rows()

    def far(slot, have):
        t = jnp.broadcast_to(s_ref[slot * ny + gy, 1:2], (8, 128))
        spread = jnp.zeros((8, 128), F32)
        for i in range(4):
            spread = jnp.where(row == i, turn(t, -32 * i, 1), spread)
        return jnp.where(have, spread, 0.0)

    outer_layers = far(jnp.maximum(gx - 2, 0), gx > 1), far(jnp.minimum(gx + 2, nx - 1), gx < nx - 2)
    level0, level1, level2 = extended(
        gx, v_ref, w_ref, v1_ref, w1_ref, v2_ref, w2_ref, al_ref, ah_ref, b_ref, outer_layers
    )

    def sides(k):
        a, b = ya_ref[k], yb_ref[k]
        return jnp.where(up, a, b), jnp.where(up, b, a)

    own = [both_ends(i, za_ref, zb_ref) for i in range(4)]
    plus, minus = zip(*(sides(12 + i) for i in range(4)))
    none = jnp.zeros((8, 128), F32)

    def outer(p, m):
        return jnp.where(row < 3, p, jnp.where(row >= 5, m, none))

    z0 = jnp.concatenate([own[0], own[1], outer(plus[0], minus[1])], axis=0)
    z1 = jnp.concatenate([own[2], outer(plus[2], minus[2])], axis=0)
    z2 = jnp.concatenate([jnp.where(row < 4, own[3], plus[3]), jnp.where(row >= 5, minus[3], none)], axis=0)

    lane16 = lanes((16, 128))
    fv[0, 0:16, 0:128] = level0[0][0]
    fv[13, 0:16, 0:128] = level0[13][0]
    for i in (0, 13):
        fv[i, 16:24, 0:128] = none
        fv[i, :, 128:256] = jnp.zeros((24, 128), F32)
    for k in range(12):
        p, m = sides(k)
        v, w = level0[k + 1]
        fv[k + 1, 0:16, 0:128] = v
        fw[k + 1, 0:16, 0:128] = w
        fv[k + 1, 16:24, 0:128] = outer(p, m)
        fw[k + 1, 16:24, 0:128] = jnp.where(row < 2, turn(p, 5, 0), jnp.where(row >= 6, turn(m, 3, 0), none))
        fv[k + 1, :, 128:256] = turn(z0, -(10 * k + 3), 1)
        fw[k + 1, :, 128:256] = turn(z0, -(10 * k + 8), 1)
        if k < 8:
            extra = outer(turn(p, 3, 0), turn(m, 5, 0))
            v, w = level1[k + 1]
            v = jnp.concatenate([v, extra], axis=0)
            w = jnp.concatenate([w, turn(extra, 64, 1)], axis=0)
            at = 10 * k + 3
            mv[k + 1] = jnp.where(lane16 < 64, v, jnp.where(lane16 < 96, turn(z1, 64 - at, 1), turn(z1, -at, 1)))
            at = 10 * k + 8
            mw[k + 1] = jnp.where(lane16 < 64, w, jnp.where(lane16 < 96, turn(z1, 64 - at, 1), turn(z1, -at, 1)))
        elif k < 11:
            near, far = turn(p, 7, 0), turn(m, 5, 0)
            for i in (0, 1):
                j = 2 * (k - 8) + i
                v, w = level2[j + 1]
                for field, target in ((0, cv), (1, cw)):
                    shift = -(64 * i + 32 * field)
                    top = jnp.where(row < 4, (v, w)[field], turn(near, shift, 1))
                    full = jnp.concatenate([top, jnp.where(row >= 5, turn(far, shift, 1), none)], axis=0)
                    at = 10 * j + (3, 8)[field]
                    ends = jnp.where(lane16 < 64, turn(z2, 32 - at, 1), turn(z2, -at, 1))
                    target[j + 1] = jnp.where(lane16 < 32, full, ends)
    for i in (0, 9):
        mv[i, 0:8] = level1[i][0]
        mv[i, 8:16] = none
    for i in (0, 7):
        cv[i, 0:8] = level2[i][0]
        cv[i, 8:16] = none

    coarse = relaxed(cv, cw, ca, cb, 8)
    s = jnp.sum(s_ref[...], axis=0)[0:1]
    plane = jnp.where(lane < 64, s / (turn(jnp.broadcast_to(s, (8, 128)), 64, 1) + 16.0), 0.0)
    src, dst = rows((128, 128)), lanes((128, 128))
    spread4 = jnp.where(src == (dst >> 2), 1.0, 0.0).astype(F32)
    spread2 = jnp.where(src == (dst >> 1), 1.0, 0.0).astype(F32)
    c = jnp.concatenate([layer[0:8] + plane for layer in coarse], axis=0)
    c = jnp.dot(c, spread4, precision=HIGHEST, preferred_element_type=F32).reshape(2, 8, 128)
    middle = relaxed(mv, mw, ma, mb, 10)
    m = jnp.concatenate([layer[0:8] for layer in middle], axis=0)
    m = jnp.dot(m, spread2, precision=HIGHEST, preferred_element_type=F32).reshape(4, 8, 128)
    for i in range(2):
        for j in range(2):
            deep_ref[i, pl.ds(j, 4, stride=2), :] = c[i, 0:4]
    for i in range(4):
        total = m[i] + deep_ref[i // 2]
        for j in range(2):
            wide_ref[i, pl.ds(j, 8, stride=2), :] = total
    fine = relaxed(fv, fw, fa, fb, 14)
    for i in range(8):
        out_ref[i] = fine[i][0:16, 0:128] + wide_ref[i // 2]


def per_device(nx, ny, nz, right_side, coefficient):
    shape = jax.ShapeDtypeStruct
    call = pl.pallas_call
    kept = [shape((8, 16, 128), F32)] * 2 + [shape((4, 8, 128), F32)] * 2 + [shape((2, 8, 128), F32)] * 2
    a_out, b_out, s_out, *own = call(
        functools.partial(first_kernel, nx, ny),
        out_shape=[shape((14, 8, 128), F32)] * 2 + [shape((nx * ny, 2, 128), F32)] + kept,
        in_specs=[VMEM],
        out_specs=[VMEM] * 9,
        scratch_shapes=[pltpu.VMEM(s, F32) for s in ((8, 16, 128), (4, 8, 128), (4, 8, 128))],
        compiler_params=pltpu.CompilerParams(vmem_limit_bytes=8 << 20),
        name="first",
    )(jnp.stack([right_side, coefficient]))
    even = lambda n: [(i, i ^ 1) for i in range(n)]
    odd = lambda n: [(i, i + 1 if i & 1 else i - 1) for i in range(1, n - 1)]
    al_in = lax.ppermute(a_out, "gx", even(nx)[: nx // 2])
    b_in = lax.ppermute(b_out, "gx", odd(nx))
    s_in = lax.all_to_all(s_out, ("gx", "gy"), 0, 0, tiled=True)
    ah_in = lax.ppermute(a_out, "gx", even(nx)[nx // 2 :])
    limit = pltpu.CompilerParams(vmem_limit_bytes=8 << 20)
    z_out, ya_own, yb_own = call(
        second_kernel,
        out_shape=[shape((4, 8, 128), F32)] + [shape((12, 8, 128), F32)] * 2,
        in_specs=[VMEM] * 9,
        out_specs=[VMEM] * 3,
        compiler_params=limit,
        name="second",
    )(*own, al_in, ah_in, b_in)
    zb_in = lax.ppermute(z_out, "gz", odd(nz))
    za_in = lax.ppermute(z_out, "gz", even(nz))
    ya_out, yb_out = call(
        third_kernel,
        out_shape=[shape((16, 8, 128), F32)] * 2,
        in_specs=[VMEM] * 4,
        out_specs=[VMEM] * 2,
        compiler_params=limit,
        name="third",
    )(za_in, zb_in, ya_own, yb_own)
    yb_in = lax.ppermute(yb_out, "gy", odd(ny))
    ya_in = lax.ppermute(ya_out, "gy", even(ny))
    fine, middle, coarse = (pltpu.VMEM(s, F32) for s in ((14, 24, 256), (10, 16, 128), (8, 16, 128)))
    return call(
        functools.partial(last_kernel, nx, ny),
        out_shape=shape((8, 16, 128), F32),
        in_specs=[VMEM] * 14,
        out_specs=VMEM,
        scratch_shapes=[fine] * 4 + [middle] * 4 + [coarse] * 4
        + [pltpu.VMEM((4, 16, 128), F32), pltpu.VMEM((2, 8, 128), F32)],
        compiler_params=pltpu.CompilerParams(vmem_limit_bytes=8 << 20),
        name="last",
    )(*own, al_in, ah_in, b_in, za_in, zb_in, ya_in, yb_in, s_in)


def solution(mesh):
    nx, ny, nz = (mesh.shape[a] for a in AXES)
    spec = P(*AXES)
    body = functools.partial(per_device, nx, ny, nz)

    return jax.shard_map(body, mesh=mesh, in_specs=(spec, spec), out_specs=spec, check_vma=False)
```

```python
import functools

import jax
import jax.numpy as jnp
from jax import lax
from jax.experimental import pallas as pl
from jax.experimental.pallas import tpu as pltpu
from jax.sharding import PartitionSpec as P


SWEEPS = 4
RELAX = 0.8
KEEP = 1.0 - RELAX
F32 = jnp.float32
VMEM = pl.BlockSpec(memory_space=pltpu.VMEM)
HIGHEST = lax.Precision.HIGHEST
AXES = ("gx", "gy", "gz")
FIRST_CHIP = 2


def along_z(chips):
    return [(i + FIRST_CHIP) % chips for i in range(chips)]


def lanes(shape=(8, 128)):
    return lax.broadcasted_iota(jnp.int32, shape, len(shape) - 1)


def rows(shape=(8, 128)):
    return lax.broadcasted_iota(jnp.int32, shape, len(shape) - 2)


def turn(x, shift, axis):
    shift = shift % x.shape[axis]
    return pltpu.roll(x, shift, axis) if shift else x


def first_kernel(
    nx, ny, in_ref, a_ref, b_ref, s_ref, v_ref, w_ref, v1_ref, w1_ref, v2_ref, w2_ref, t_ref, u_ref, d_ref,
):
    gx = lax.axis_index("gx")
    r, c = in_ref[0], in_ref[1]
    w = RELAX / (6.0 + c)
    v = w * r
    v_ref[...] = v
    w_ref[...] = w
    r4, c4 = r.reshape(4, 2, 16, 128), c.reshape(4, 2, 16, 128)
    t_ref[0:4] = r4[:, 0] + r4[:, 1]
    t_ref[4:8] = c4[:, 0] + c4[:, 1]
    a = t_ref[:, pl.ds(0, 8, stride=2), :] + t_ref[:, pl.ds(1, 8, stride=2), :]
    src, dst = rows((128, 128)), lanes((128, 128))
    half = jnp.where((src >> 1) == (dst & 63), 0.125, 0.0).astype(F32)
    one = jnp.dot(a.reshape(64, 128), half, precision=HIGHEST, preferred_element_type=F32)
    r1, c1 = one[:32].reshape(4, 8, 128), one[32:].reshape(4, 8, 128)
    d1 = RELAX / (1.5 + c1)
    v1, w1 = d1 * r1, d1 * 0.25
    v1_ref[...] = v1
    w1_ref[...] = w1
    a4 = a.reshape(4, 2, 8, 128)
    u_ref[...] = a4[:, 0] + a4[:, 1]
    e = u_ref[:, pl.ds(0, 4, stride=2), :] + u_ref[:, pl.ds(1, 4, stride=2), :]
    d_ref[:, 0:4, :] = e
    d_ref[:, 4:8, :] = e
    quarter = jnp.where((src >> 2) == (dst & 31), 0.015625, 0.0).astype(F32)
    two = jnp.dot(d_ref[...].reshape(32, 128), quarter, precision=HIGHEST, preferred_element_type=F32)
    r2, c2 = two[:16].reshape(2, 8, 128), two[16:].reshape(2, 8, 128)
    d2 = RELAX / (0.375 + c2)
    v2, w2 = d2 * r2, d2 * 0.0625
    v2_ref[...] = v2
    w2_ref[...] = w2
    lane, row = lanes(), rows()
    low = lane < 64
    sums = jnp.where(low, r2[0] + r2[1], c2[0] + c2[1])
    sums = 0.5 * jnp.sum(sums, axis=0, keepdims=True)
    quad = (lane & 63) < 32
    both = [jnp.where(quad, v2[i], w2[i]) for i in (0, 1)]
    last = jnp.where(row < 4, both[0], both[1])
    ends = [jnp.sum(jnp.where((lane >> 5) == row, v2[i], 0.0), axis=0, keepdims=True) for i in (0, 1)]
    mails = []
    for j in range(nx):
        mails.append(jnp.concatenate([sums, jnp.where(j > gx, ends[1], ends[0])], axis=0))
    for i, z in enumerate(along_z(nx * ny // 2)):
        for core in (1, 0):
            s_ref[2 * i + 1 - core] = mails[2 * (z // ny) + core]
    even = (gx & 1) == 0
    for x_ref, up in ((a_ref, even), (b_ref, jnp.logical_not(even))):
        for d in range(3):
            face = jnp.where(up, v[7 - d], v[d])
            x_ref[2 * d] = face[0:8]
            x_ref[2 * d + 1] = face[8:16]
        for d in range(2):
            face = jnp.where(up, w[7 - d], w[d])
            x_ref[6 + 2 * d] = face[0:8]
            x_ref[7 + 2 * d] = face[8:16]
        for d in range(3):
            x_ref[10 + d] = jnp.where(low, jnp.where(up, v1[3 - d], v1[d]), jnp.where(up, w1[3 - d], w1[d]))
        x_ref[13] = last


def extended(gx, v_ref, w_ref, v1_ref, w1_ref, v2_ref, w2_ref, al_ref, ah_ref, b_ref, far=(None, None)):
    lane, row = lanes(), rows()
    low = lane < 64
    quad = (lane & 63) < 32
    even = (gx & 1) == 0
    near = lambda tile: al_ref[tile] + ah_ref[tile]
    left = lambda tile: jnp.where(even, b_ref[tile], near(tile))
    right = lambda tile: jnp.where(even, near(tile), b_ref[tile])

    def pair(side, tile):
        return jnp.concatenate([side(tile), side(tile + 1)], axis=0)

    def fine(side, d):
        return pair(side, 2 * d), (pair(side, 6 + 2 * d) if d < 2 else None)

    def middle(side, d):
        t = side(10 + d)
        s = turn(t, 64, 1)
        return jnp.where(low, t, s), jnp.where(low, s, t)

    def coarse(side, layer):
        t = side(13)
        s = turn(t, 4, 0)
        t = jnp.where(row < 4, t, s) if layer == 0 else jnp.where(row < 4, s, t)
        s = turn(t, 32, 1)
        return jnp.where(quad, t, s), jnp.where(quad, s, t)

    level0 = (
        [fine(left, d) for d in (2, 1, 0)]
        + [(v_ref[i], w_ref[i]) for i in range(8)]
        + [fine(right, d) for d in (0, 1, 2)]
    )
    level1 = (
        [middle(left, d) for d in (2, 1, 0)]
        + [(v1_ref[i], w1_ref[i]) for i in range(4)]
        + [middle(right, d) for d in (0, 1, 2)]
    )
    level2 = (
        [(far[0], None), coarse(left, 0), coarse(left, 1)]
        + [(v2_ref[i], w2_ref[i]) for i in range(2)]
        + [coarse(right, 0), coarse(right, 1), (far[1], None)]
    )
    return level0, level1, level2


def edge_lanes(layers):
    shape = layers[0][0].shape
    lane = lanes(shape)
    packed = jnp.zeros(shape, F32)
    for k, (v, w) in enumerate(layers):
        at = 10 * k
        packed = jnp.where((lane >= at) & (lane < at + 6), turn(v, at + 3, 1), packed)
        packed = jnp.where((lane >= at + 6) & (lane < at + 10), turn(w, at + 8, 1), packed)
    return packed


def second_kernel(v_ref, w_ref, v1_ref, w1_ref, v2_ref, w2_ref, al_ref, ah_ref, b_ref, z_ref, ya_ref, yb_ref):
    gx, gy = lax.axis_index("gx"), lax.axis_index("gy")
    level0, level1, level2 = extended(gx, v_ref, w_ref, v1_ref, w1_ref, v2_ref, w2_ref, al_ref, ah_ref, b_ref)
    lane, row = lanes(), rows()
    low = lane < 64
    quad = (lane & 63) < 32
    up = (gy & 1) == 0
    ends = edge_lanes(level0[1:13])
    for i, tile in enumerate((ends[0:8], ends[8:16], edge_lanes(level1[1:9]), edge_lanes(level2[1:7]))):
        z_ref[i] = tile
    for k in range(12):
        v, w = level0[k + 1]
        if k < 8:
            a, b = level1[k + 1]
            extra = jnp.where(low, a, b)
        elif k < 11:
            a, b = (jnp.where(quad, *level2[1 + 2 * (k - 8) + i]) for i in (0, 1))
            extra = jnp.where(low, a, b)
        else:
            extra = jnp.zeros((8, 128), F32)
        high = jnp.where(row >= 5, v[8:16], jnp.where(row >= 3, turn(w[8:16], 5, 0), turn(extra, 3, 0)))
        base = jnp.where(row < 3, v[0:8], jnp.where(row < 5, turn(w[0:8], 3, 0), turn(extra, 5, 0)))
        ya_ref[k] = jnp.where(up, high, base)
        yb_ref[k] = jnp.where(up, base, high)


def both_ends(i, za_ref, zb_ref):
    lane = lanes()
    part = lane - 10 * (lane // 10)
    ahead = (lax.axis_index("gz") & 1) == 0
    last = (part < 3) | ((part >= 6) & (part < 8))
    from_a = jnp.where(ahead, jnp.where(last, 0, 1), jnp.where(last, 1, 0)) == 1
    return jnp.where(from_a, za_ref[i], zb_ref[i])


def third_kernel(za_ref, zb_ref, ya_ref, yb_ref, ya_out, yb_out):
    ya_out[0:12] = ya_ref[...]
    yb_out[0:12] = yb_ref[...]
    for i in range(4):
        ends = both_ends(i, za_ref, zb_ref)
        ya_out[12 + i] = ends
        yb_out[12 + i] = ends


def around(v, above, below):
    return (
        above
        + below
        + turn(v, 1, 0)
        + turn(v, -1, 0)
        + turn(v, 1, 1)
        + turn(v, -1, 1)
    )


def relaxed(v_ref, w_ref, a_ref, b_ref, count):
    done = []
    for sweep in range(SWEEPS - 1):
        source = (v_ref, a_ref, b_ref)[sweep]
        target = (a_ref, b_ref, None)[sweep]
        for i in range(sweep + 1, count - sweep - 1):
            v = source[i]
            new = KEEP * v + v_ref[i] + w_ref[i] * around(v, source[i - 1], source[i + 1])
            if target is None:
                done.append(new)
            else:
                target[i] = new
    return done


def last_kernel(
    nx, ny, v_ref, w_ref, v1_ref, w1_ref, v2_ref, w2_ref, al_ref, ah_ref, b_ref, za_ref, zb_ref, ya_ref, yb_ref, s_ref, out_ref,
    fv, fw, fa, fb, mv, mw, ma, mb, cv, cw, ca, cb, wide_ref, deep_ref,
):
    gx, gy = lax.axis_index("gx"), lax.axis_index("gy")
    up = (gy & 1) == 0
    lane, row = lanes(), rows()

    def far(slot, have):
        chips = nx * ny // 2
        place = lax.rem((slot >> 1) * ny + gy + chips - FIRST_CHIP, chips)
        t = jnp.broadcast_to(s_ref[2 * place + 1 - (slot & 1), 1:2], (8, 128))
        spread = jnp.zeros((8, 128), F32)
        for i in range(4):
            spread = jnp.where(row == i, turn(t, -32 * i, 1), spread)
        return jnp.where(have, spread, 0.0)

    outer_layers = far(jnp.maximum(gx - 2, 0), gx > 1), far(jnp.minimum(gx + 2, nx - 1), gx < nx - 2)
    level0, level1, level2 = extended(
        gx, v_ref, w_ref, v1_ref, w1_ref, v2_ref, w2_ref, al_ref, ah_ref, b_ref, outer_layers
    )

    def sides(k):
        a, b = ya_ref[k], yb_ref[k]
        return jnp.where(up, a, b), jnp.where(up, b, a)

    own = [both_ends(i, za_ref, zb_ref) for i in range(4)]
    plus, minus = zip(*(sides(12 + i) for i in range(4)))
    none = jnp.zeros((8, 128), F32)

    def outer(p, m):
        return jnp.where(row < 3, p, jnp.where(row >= 5, m, none))

    z0 = jnp.concatenate([own[0], own[1], outer(plus[0], minus[1])], axis=0)
    z1 = jnp.concatenate([own[2], outer(plus[2], minus[2])], axis=0)
    z2 = jnp.concatenate([jnp.where(row < 4, own[3], plus[3]), jnp.where(row >= 5, minus[3], none)], axis=0)

    lane16 = lanes((16, 128))
    fv[0, 0:16, 0:128] = level0[0][0]
    fv[13, 0:16, 0:128] = level0[13][0]
    for i in (0, 13):
        fv[i, 16:24, 0:128] = none
        fv[i, :, 128:256] = jnp.zeros((24, 128), F32)
    for k in range(12):
        p, m = sides(k)
        v, w = level0[k + 1]
        fv[k + 1, 0:16, 0:128] = v
        fw[k + 1, 0:16, 0:128] = w
        fv[k + 1, 16:24, 0:128] = outer(p, m)
        fw[k + 1, 16:24, 0:128] = jnp.where(row < 2, turn(p, 5, 0), jnp.where(row >= 6, turn(m, 3, 0), none))
        fv[k + 1, :, 128:256] = turn(z0, -(10 * k + 3), 1)
        fw[k + 1, :, 128:256] = turn(z0, -(10 * k + 8), 1)
        if k < 8:
            extra = outer(turn(p, 3, 0), turn(m, 5, 0))
            v, w = level1[k + 1]
            v = jnp.concatenate([v, extra], axis=0)
            w = jnp.concatenate([w, turn(extra, 64, 1)], axis=0)
            at = 10 * k + 3
            mv[k + 1] = jnp.where(lane16 < 64, v, jnp.where(lane16 < 96, turn(z1, 64 - at, 1), turn(z1, -at, 1)))
            at = 10 * k + 8
            mw[k + 1] = jnp.where(lane16 < 64, w, jnp.where(lane16 < 96, turn(z1, 64 - at, 1), turn(z1, -at, 1)))
        elif k < 11:
            near, far = turn(p, 7, 0), turn(m, 5, 0)
            for i in (0, 1):
                j = 2 * (k - 8) + i
                v, w = level2[j + 1]
                for field, target in ((0, cv), (1, cw)):
                    shift = -(64 * i + 32 * field)
                    top = jnp.where(row < 4, (v, w)[field], turn(near, shift, 1))
                    full = jnp.concatenate([top, jnp.where(row >= 5, turn(far, shift, 1), none)], axis=0)
                    at = 10 * j + (3, 8)[field]
                    ends = jnp.where(lane16 < 64, turn(z2, 32 - at, 1), turn(z2, -at, 1))
                    target[j + 1] = jnp.where(lane16 < 32, full, ends)
    for i in (0, 9):
        mv[i, 0:8] = level1[i][0]
        mv[i, 8:16] = none
    for i in (0, 7):
        cv[i, 0:8] = level2[i][0]
        cv[i, 8:16] = none

    coarse = relaxed(cv, cw, ca, cb, 8)
    s = jnp.sum(s_ref[...], axis=0)[0:1]
    plane = jnp.where(lane < 64, s / (turn(jnp.broadcast_to(s, (8, 128)), 64, 1) + 16.0), 0.0)
    src, dst = rows((128, 128)), lanes((128, 128))
    spread4 = jnp.where(src == (dst >> 2), 1.0, 0.0).astype(F32)
    spread2 = jnp.where(src == (dst >> 1), 1.0, 0.0).astype(F32)
    c = jnp.concatenate([layer[0:8] + plane for layer in coarse], axis=0)
    c = jnp.dot(c, spread4, precision=HIGHEST, preferred_element_type=F32).reshape(2, 8, 128)
    middle = relaxed(mv, mw, ma, mb, 10)
    m = jnp.concatenate([layer[0:8] for layer in middle], axis=0)
    m = jnp.dot(m, spread2, precision=HIGHEST, preferred_element_type=F32).reshape(4, 8, 128)
    for i in range(2):
        for j in range(2):
            deep_ref[i, pl.ds(j, 4, stride=2), :] = c[i, 0:4]
    for i in range(4):
        total = m[i] + deep_ref[i // 2]
        for j in range(2):
            wide_ref[i, pl.ds(j, 8, stride=2), :] = total
    fine = relaxed(fv, fw, fa, fb, 14)
    for i in range(8):
        out_ref[i] = fine[i][0:16, 0:128] + wide_ref[i // 2]


def per_device(nx, ny, nz, right_side, coefficient):
    shape = jax.ShapeDtypeStruct
    call = pl.pallas_call
    kept = [shape((8, 16, 128), F32)] * 2 + [shape((4, 8, 128), F32)] * 2 + [shape((2, 8, 128), F32)] * 2
    a_out, b_out, s_out, *own = call(
        functools.partial(first_kernel, nx, ny),
        out_shape=[shape((14, 8, 128), F32)] * 2 + [shape((nx * ny, 2, 128), F32)] + kept,
        in_specs=[VMEM],
        out_specs=[VMEM] * 9,
        scratch_shapes=[pltpu.VMEM(s, F32) for s in ((8, 16, 128), (4, 8, 128), (4, 8, 128))],
        compiler_params=pltpu.CompilerParams(vmem_limit_bytes=8 << 20),
        name="first",
    )(jnp.stack([right_side, coefficient]))
    even = lambda n: [(i, i ^ 1) for i in range(n)]
    odd = lambda n: [(i, i + 1 if i & 1 else i - 1) for i in range(1, n - 1)]
    al_in = lax.ppermute(a_out, "gx", even(nx)[: nx // 2])
    b_in = lax.ppermute(b_out, "gx", odd(nx))
    ring = [(2 * (z // ny) + core) * ny + z % ny for z in along_z(nx * ny // 2) for core in (1, 0)]
    s_in = lax.all_to_all(s_out, ("gx", "gy"), 0, 0, tiled=True, axis_index_groups=[ring])
    ah_in = lax.ppermute(a_out, "gx", even(nx)[nx // 2 :])
    limit = pltpu.CompilerParams(vmem_limit_bytes=8 << 20)
    z_out, ya_own, yb_own = call(
        second_kernel,
        out_shape=[shape((4, 8, 128), F32)] + [shape((12, 8, 128), F32)] * 2,
        in_specs=[VMEM] * 9,
        out_specs=[VMEM] * 3,
        compiler_params=limit,
        name="second",
    )(*own, al_in, ah_in, b_in)
    zb_in = lax.ppermute(z_out, "gz", odd(nz))
    za_in = lax.ppermute(z_out, "gz", even(nz))
    ya_out, yb_out = call(
        third_kernel,
        out_shape=[shape((16, 8, 128), F32)] * 2,
        in_specs=[VMEM] * 4,
        out_specs=[VMEM] * 2,
        compiler_params=limit,
        name="third",
    )(za_in, zb_in, ya_own, yb_own)
    yb_in = lax.ppermute(yb_out, "gy", odd(ny))
    ya_in = lax.ppermute(ya_out, "gy", even(ny))
    fine, middle, coarse = (pltpu.VMEM(s, F32) for s in ((14, 24, 256), (10, 16, 128), (8, 16, 128)))
    return call(
        functools.partial(last_kernel, nx, ny),
        out_shape=shape((8, 16, 128), F32),
        in_specs=[VMEM] * 14,
        out_specs=VMEM,
        scratch_shapes=[fine] * 4 + [middle] * 4 + [coarse] * 4
        + [pltpu.VMEM((4, 16, 128), F32), pltpu.VMEM((2, 8, 128), F32)],
        compiler_params=pltpu.CompilerParams(vmem_limit_bytes=8 << 20),
        name="last",
    )(*own, al_in, ah_in, b_in, za_in, zb_in, ya_in, yb_in, s_in)


def solution(mesh):
    nx, ny, nz = (mesh.shape[a] for a in AXES)
    spec = P(*AXES)
    body = functools.partial(per_device, nx, ny, nz)

    return jax.shard_map(body, mesh=mesh, in_specs=(spec, spec), out_specs=spec, check_vma=False)
```

```python
import functools

import jax
import jax.numpy as jnp
from jax import lax
from jax.experimental import pallas as pl
from jax.experimental.pallas import tpu as pltpu
from jax.sharding import PartitionSpec as P


SWEEPS = 4
RELAX = 0.8
KEEP = 1.0 - RELAX
F32 = jnp.float32
VMEM = pl.BlockSpec(memory_space=pltpu.VMEM)
HIGHEST = lax.Precision.HIGHEST
AXES = ("gx", "gy", "gz")
FIRST_CHIP = 2


def along_z(chips):
    return [(i + FIRST_CHIP) % chips for i in range(chips)]


def lanes(shape=(8, 128)):
    return lax.broadcasted_iota(jnp.int32, shape, len(shape) - 1)


def rows(shape=(8, 128)):
    return lax.broadcasted_iota(jnp.int32, shape, len(shape) - 2)


def turn(x, shift, axis):
    shift = shift % x.shape[axis]
    return pltpu.roll(x, shift, axis) if shift else x


def first_kernel(
    nx, ny, in_ref, a_ref, b_ref, s_ref, v_ref, w_ref, v1_ref, w1_ref, v2_ref, w2_ref, t_ref, u_ref, d_ref,
):
    gx = lax.axis_index("gx")
    r, c = in_ref[0], in_ref[1]
    w = RELAX / (6.0 + c)
    v = w * r
    v_ref[...] = v
    w_ref[...] = w
    r4, c4 = r.reshape(4, 2, 16, 128), c.reshape(4, 2, 16, 128)
    t_ref[0:4] = r4[:, 0] + r4[:, 1]
    t_ref[4:8] = c4[:, 0] + c4[:, 1]
    a = t_ref[:, pl.ds(0, 8, stride=2), :] + t_ref[:, pl.ds(1, 8, stride=2), :]
    src, dst = rows((128, 128)), lanes((128, 128))
    half = jnp.where((src >> 1) == (dst & 63), 0.125, 0.0).astype(F32)
    one = jnp.dot(a.reshape(64, 128), half, precision=HIGHEST, preferred_element_type=F32)
    r1, c1 = one[:32].reshape(4, 8, 128), one[32:].reshape(4, 8, 128)
    d1 = RELAX / (1.5 + c1)
    v1, w1 = d1 * r1, d1 * 0.25
    v1_ref[...] = v1
    w1_ref[...] = w1
    a4 = a.reshape(4, 2, 8, 128)
    u_ref[...] = a4[:, 0] + a4[:, 1]
    e = u_ref[:, pl.ds(0, 4, stride=2), :] + u_ref[:, pl.ds(1, 4, stride=2), :]
    d_ref[:, 0:4, :] = e
    d_ref[:, 4:8, :] = e
    quarter = jnp.where((src >> 2) == (dst & 31), 0.015625, 0.0).astype(F32)
    two = jnp.dot(d_ref[...].reshape(32, 128), quarter, precision=HIGHEST, preferred_element_type=F32)
    r2, c2 = two[:16].reshape(2, 8, 128), two[16:].reshape(2, 8, 128)
    d2 = RELAX / (0.375 + c2)
    v2, w2 = d2 * r2, d2 * 0.0625
    v2_ref[...] = v2
    w2_ref[...] = w2
    lane, row = lanes(), rows()
    low = lane < 64
    sums = jnp.where(low, r2[0] + r2[1], c2[0] + c2[1])
    sums = 0.5 * jnp.sum(sums, axis=0, keepdims=True)
    quad = (lane & 63) < 32
    both = [jnp.where(quad, v2[i], w2[i]) for i in (0, 1)]
    last = jnp.where(row < 4, both[0], both[1])
    ends = [jnp.sum(jnp.where((lane >> 5) == row, v2[i], 0.0), axis=0, keepdims=True) for i in (0, 1)]
    mails = []
    for j in range(nx):
        mails.append(jnp.concatenate([sums, jnp.where(j > gx, ends[1], ends[0])], axis=0))
    for i, z in enumerate(along_z(nx * ny // 2)):
        for core in (1, 0):
            s_ref[2 * i + 1 - core] = mails[2 * (z // ny) + core]
    even = (gx & 1) == 0
    for x_ref, up in ((a_ref, even), (b_ref, jnp.logical_not(even))):
        for d in range(3):
            face = jnp.where(up, v[7 - d], v[d])
            x_ref[2 * d] = face[0:8]
            x_ref[2 * d + 1] = face[8:16]
        for d in range(2):
            face = jnp.where(up, w[7 - d], w[d])
            x_ref[6 + 2 * d] = face[0:8]
            x_ref[7 + 2 * d] = face[8:16]
        for d in range(3):
            x_ref[10 + d] = jnp.where(low, jnp.where(up, v1[3 - d], v1[d]), jnp.where(up, w1[3 - d], w1[d]))
        x_ref[13] = last


def extended(gx, v_ref, w_ref, v1_ref, w1_ref, v2_ref, w2_ref, al_ref, ah_ref, b_ref, far=(None, None)):
    lane, row = lanes(), rows()
    low = lane < 64
    quad = (lane & 63) < 32
    even = (gx & 1) == 0
    near = lambda tile: al_ref[tile] + ah_ref[tile]
    left = lambda tile: jnp.where(even, b_ref[tile], near(tile))
    right = lambda tile: jnp.where(even, near(tile), b_ref[tile])

    def pair(side, tile):
        return jnp.concatenate([side(tile), side(tile + 1)], axis=0)

    def fine(side, d):
        return pair(side, 2 * d), (pair(side, 6 + 2 * d) if d < 2 else None)

    def middle(side, d):
        t = side(10 + d)
        s = turn(t, 64, 1)
        return jnp.where(low, t, s), jnp.where(low, s, t)

    def coarse(side, layer):
        t = side(13)
        s = turn(t, 4, 0)
        t = jnp.where(row < 4, t, s) if layer == 0 else jnp.where(row < 4, s, t)
        s = turn(t, 32, 1)
        return jnp.where(quad, t, s), jnp.where(quad, s, t)

    level0 = (
        [fine(left, d) for d in (2, 1, 0)]
        + [(v_ref[i], w_ref[i]) for i in range(8)]
        + [fine(right, d) for d in (0, 1, 2)]
    )
    level1 = (
        [middle(left, d) for d in (2, 1, 0)]
        + [(v1_ref[i], w1_ref[i]) for i in range(4)]
        + [middle(right, d) for d in (0, 1, 2)]
    )
    level2 = (
        [(far[0], None), coarse(left, 0), coarse(left, 1)]
        + [(v2_ref[i], w2_ref[i]) for i in range(2)]
        + [coarse(right, 0), coarse(right, 1), (far[1], None)]
    )
    return level0, level1, level2


def edge_lanes(layers):
    shape = layers[0][0].shape
    lane = lanes(shape)
    packed = jnp.zeros(shape, F32)
    for k, (v, w) in enumerate(layers):
        at = 10 * k
        packed = jnp.where((lane >= at) & (lane < at + 6), turn(v, at + 3, 1), packed)
        packed = jnp.where((lane >= at + 6) & (lane < at + 10), turn(w, at + 8, 1), packed)
    return packed


def second_kernel(v_ref, w_ref, v1_ref, w1_ref, v2_ref, w2_ref, al_ref, ah_ref, b_ref, z_ref, ya_ref, yb_ref):
    gx, gy = lax.axis_index("gx"), lax.axis_index("gy")
    level0, level1, level2 = extended(gx, v_ref, w_ref, v1_ref, w1_ref, v2_ref, w2_ref, al_ref, ah_ref, b_ref)
    lane, row = lanes(), rows()
    low = lane < 64
    quad = (lane & 63) < 32
    up = (gy & 1) == 0
    ends = edge_lanes(level0[1:13])
    for i, tile in enumerate((ends[0:8], ends[8:16], edge_lanes(level1[1:9]), edge_lanes(level2[1:7]))):
        z_ref[i] = tile
    for k in range(12):
        v, w = level0[k + 1]
        if k < 8:
            a, b = level1[k + 1]
            extra = jnp.where(low, a, b)
        elif k < 11:
            a, b = (jnp.where(quad, *level2[1 + 2 * (k - 8) + i]) for i in (0, 1))
            extra = jnp.where(low, a, b)
        else:
            extra = jnp.zeros((8, 128), F32)
        high = jnp.where(row >= 5, v[8:16], jnp.where(row >= 3, turn(w[8:16], 5, 0), turn(extra, 3, 0)))
        base = jnp.where(row < 3, v[0:8], jnp.where(row < 5, turn(w[0:8], 3, 0), turn(extra, 5, 0)))
        ya_ref[k] = jnp.where(up, high, base)
        yb_ref[k] = jnp.where(up, base, high)


def both_ends(i, za_ref, zb_ref):
    lane = lanes()
    part = lane - 10 * (lane // 10)
    ahead = (lax.axis_index("gz") & 1) == 0
    last = (part < 3) | ((part >= 6) & (part < 8))
    from_a = jnp.where(ahead, jnp.where(last, 0, 1), jnp.where(last, 1, 0)) == 1
    return jnp.where(from_a, za_ref[i], zb_ref[i])


def third_kernel(za_ref, zb_ref, ya_ref, yb_ref, ya_out, yb_out):
    ya_out[0:12] = ya_ref[...]
    yb_out[0:12] = yb_ref[...]
    for i in range(4):
        ends = both_ends(i, za_ref, zb_ref)
        ya_out[12 + i] = ends
        yb_out[12 + i] = ends


def around(v, above, below):
    return (
        above
        + below
        + turn(v, 1, 0)
        + turn(v, -1, 0)
        + turn(v, 1, 1)
        + turn(v, -1, 1)
    )


def relaxed(start, weight, a_ref, b_ref, count):
    done = []
    for sweep in range(SWEEPS - 1):
        source = (start, lambda i: a_ref[i], lambda i: b_ref[i])[sweep]
        target = (a_ref, b_ref, None)[sweep]
        for i in range(sweep + 1, count - sweep - 1):
            v = source(i)
            new = KEEP * v + start(i) + weight(i) * around(v, source(i - 1), source(i + 1))
            if target is None:
                done.append(new)
            else:
                target[i] = new
    return done


def fourth_kernel(
    v_ref, w_ref, v1_ref, w1_ref, v2_ref, w2_ref, al_ref, ah_ref, b_ref, za_ref, zb_ref, fv, fw, mv, mw
):
    level0, level1, _ = extended(
        lax.axis_index("gx"), v_ref, w_ref, v1_ref, w1_ref, v2_ref, w2_ref, al_ref, ah_ref, b_ref
    )
    own = [both_ends(i, za_ref, zb_ref) for i in range(3)]
    z0, lane = jnp.concatenate(own[0:2], axis=0), lanes()
    for i in range(14):
        v, w = level0[i]
        fv[i, :, 0:128] = v
        if 1 <= i < 13:
            fw[i, :, 0:128] = w
            fv[i, :, 128:256] = turn(z0, -(10 * i - 7), 1)
            fw[i, :, 128:256] = turn(z0, -(10 * i - 2), 1)
        else:
            fv[i, :, 128:256] = jnp.zeros((16, 128), F32)
    for i in range(10):
        if 1 <= i < 9:
            for field, target, at in ((0, mv, 10 * i - 7), (1, mw, 10 * i - 2)):
                ends = jnp.where(lane < 96, turn(own[2], 64 - at, 1), turn(own[2], -at, 1))
                target[i] = jnp.where(lane < 64, level1[i][field], ends)
        else:
            mv[i] = level1[i][0]


def last_kernel(
    nx, ny, v_ref, w_ref, v1_ref, w1_ref, v2_ref, w2_ref, al_ref, ah_ref, b_ref, za_ref, zb_ref,
    fv_ref, fw_ref, mv_ref, mw_ref, ya_ref, yb_ref, s_ref, out_ref,
    fv, fw, fa, fb, mv, mw, ma, mb, cv, cw, ca, cb, wide_ref, deep_ref,
):
    gx, gy = lax.axis_index("gx"), lax.axis_index("gy")
    up = (gy & 1) == 0
    lane, row = lanes(), rows()

    def far(slot, have):
        chips = nx * ny // 2
        place = lax.rem((slot >> 1) * ny + gy + chips - FIRST_CHIP, chips)
        t = jnp.broadcast_to(s_ref[2 * place + 1 - (slot & 1), 1:2], (8, 128))
        spread = jnp.zeros((8, 128), F32)
        for i in range(4):
            spread = jnp.where(row == i, turn(t, -32 * i, 1), spread)
        return jnp.where(have, spread, 0.0)

    outer_layers = far(jnp.maximum(gx - 2, 0), gx > 1), far(jnp.minimum(gx + 2, nx - 1), gx < nx - 2)
    _, _, level2 = extended(
        gx, v_ref, w_ref, v1_ref, w1_ref, v2_ref, w2_ref, al_ref, ah_ref, b_ref, outer_layers
    )

    def sides(k):
        a, b = ya_ref[k], yb_ref[k]
        return jnp.where(up, a, b), jnp.where(up, b, a)

    own = both_ends(3, za_ref, zb_ref)
    plus, minus = zip(*(sides(12 + i) for i in range(4)))
    none = jnp.zeros((8, 128), F32)

    def outer(p, m):
        return jnp.where(row < 3, p, jnp.where(row >= 5, m, none))

    z0 = outer(plus[0], minus[1])
    z1 = outer(plus[2], minus[2])
    z2 = jnp.concatenate([jnp.where(row < 4, own, plus[3]), jnp.where(row >= 5, minus[3], none)], axis=0)

    lane16 = lanes((16, 128))
    for i in (0, 13):
        fv[i] = jnp.zeros((8, 256), F32)
    for i in (0, 9):
        mv[i] = none
    for k in range(12):
        p, m = sides(k)
        fv[k + 1, :, 0:128] = outer(p, m)
        fw[k + 1, :, 0:128] = jnp.where(row < 2, turn(p, 5, 0), jnp.where(row >= 6, turn(m, 3, 0), none))
        fv[k + 1, :, 128:256] = turn(z0, -(10 * k + 3), 1)
        fw[k + 1, :, 128:256] = turn(z0, -(10 * k + 8), 1)
        if k < 8:
            extra = outer(turn(p, 3, 0), turn(m, 5, 0))
            for field, target, at in ((extra, mv, 10 * k + 3), (turn(extra, 64, 1), mw, 10 * k + 8)):
                ends = jnp.where(lane < 96, turn(z1, 64 - at, 1), turn(z1, -at, 1))
                target[k + 1] = jnp.where(lane < 64, field, ends)
        elif k < 11:
            near, far = turn(p, 7, 0), turn(m, 5, 0)
            for i in (0, 1):
                j = 2 * (k - 8) + i
                v, w = level2[j + 1]
                for field, target in ((0, cv), (1, cw)):
                    shift = -(64 * i + 32 * field)
                    top = jnp.where(row < 4, (v, w)[field], turn(near, shift, 1))
                    full = jnp.concatenate([top, jnp.where(row >= 5, turn(far, shift, 1), none)], axis=0)
                    at = 10 * j + (3, 8)[field]
                    ends = jnp.where(lane16 < 64, turn(z2, 32 - at, 1), turn(z2, -at, 1))
                    target[j + 1] = jnp.where(lane16 < 32, full, ends)
    for i in (0, 7):
        cv[i, 0:8] = level2[i][0]
        cv[i, 8:16] = none

    joined = lambda near_ref, far_ref: lambda i: jnp.concatenate([near_ref[i], far_ref[i]], axis=0)
    coarse = relaxed(lambda i: cv[i], lambda i: cw[i], ca, cb, 8)
    s = jnp.sum(s_ref[...], axis=0)[0:1]
    plane = jnp.where(lane < 64, s / (turn(jnp.broadcast_to(s, (8, 128)), 64, 1) + 16.0), 0.0)
    src, dst = rows((128, 128)), lanes((128, 128))
    spread4 = jnp.where(src == (dst >> 2), 1.0, 0.0).astype(F32)
    spread2 = jnp.where(src == (dst >> 1), 1.0, 0.0).astype(F32)
    c = jnp.concatenate([layer[0:8] + plane for layer in coarse], axis=0)
    c = jnp.dot(c, spread4, precision=HIGHEST, preferred_element_type=F32).reshape(2, 8, 128)
    middle = relaxed(joined(mv_ref, mv), joined(mw_ref, mw), ma, mb, 10)
    m = jnp.concatenate([layer[0:8] for layer in middle], axis=0)
    m = jnp.dot(m, spread2, precision=HIGHEST, preferred_element_type=F32).reshape(4, 8, 128)
    for i in range(2):
        for j in range(2):
            deep_ref[i, pl.ds(j, 4, stride=2), :] = c[i, 0:4]
    for i in range(4):
        total = m[i] + deep_ref[i // 2]
        for j in range(2):
            wide_ref[i, pl.ds(j, 8, stride=2), :] = total
    fine = relaxed(joined(fv_ref, fv), joined(fw_ref, fw), fa, fb, 14)
    for i in range(8):
        out_ref[i] = fine[i][0:16, 0:128] + wide_ref[i // 2]


def per_device(nx, ny, nz, right_side, coefficient):
    shape = jax.ShapeDtypeStruct
    call = pl.pallas_call
    kept = [shape((8, 16, 128), F32)] * 2 + [shape((4, 8, 128), F32)] * 2 + [shape((2, 8, 128), F32)] * 2
    a_out, b_out, s_out, *own = call(
        functools.partial(first_kernel, nx, ny),
        out_shape=[shape((14, 8, 128), F32)] * 2 + [shape((nx * ny, 2, 128), F32)] + kept,
        in_specs=[VMEM],
        out_specs=[VMEM] * 9,
        scratch_shapes=[pltpu.VMEM(s, F32) for s in ((8, 16, 128), (4, 8, 128), (4, 8, 128))],
        compiler_params=pltpu.CompilerParams(vmem_limit_bytes=8 << 20),
        name="first",
    )(jnp.stack([right_side, coefficient]))
    even = lambda n: [(i, i ^ 1) for i in range(n)]
    odd = lambda n: [(i, i + 1 if i & 1 else i - 1) for i in range(1, n - 1)]
    al_in = lax.ppermute(a_out, "gx", even(nx)[: nx // 2])
    b_in = lax.ppermute(b_out, "gx", odd(nx))
    ring = [(2 * (z // ny) + core) * ny + z % ny for z in along_z(nx * ny // 2) for core in (1, 0)]
    s_in = lax.all_to_all(s_out, ("gx", "gy"), 0, 0, tiled=True, axis_index_groups=[ring])
    ah_in = lax.ppermute(a_out, "gx", even(nx)[nx // 2 :])
    limit = pltpu.CompilerParams(vmem_limit_bytes=8 << 20)
    z_out, ya_own, yb_own = call(
        second_kernel,
        out_shape=[shape((4, 8, 128), F32)] + [shape((12, 8, 128), F32)] * 2,
        in_specs=[VMEM] * 9,
        out_specs=[VMEM] * 3,
        compiler_params=limit,
        name="second",
    )(*own, al_in, ah_in, b_in)
    zb_in = lax.ppermute(z_out, "gz", odd(nz))
    za_in = lax.ppermute(z_out, "gz", even(nz))
    ya_out, yb_out = call(
        third_kernel,
        out_shape=[shape((16, 8, 128), F32)] * 2,
        in_specs=[VMEM] * 4,
        out_specs=[VMEM] * 2,
        compiler_params=limit,
        name="third",
    )(za_in, zb_in, ya_own, yb_own)
    yb_in = lax.ppermute(yb_out, "gy", odd(ny))
    ya_in = lax.ppermute(ya_out, "gy", even(ny))
    rows_own = call(
        fourth_kernel,
        out_shape=[shape((14, 16, 256), F32)] * 2 + [shape((10, 8, 128), F32)] * 2,
        in_specs=[VMEM] * 11,
        out_specs=[VMEM] * 4,
        compiler_params=limit,
        name="fourth",
    )(*own, al_in, ah_in, b_in, za_in, zb_in)
    edge, fine, thin, middle, coarse = (
        pltpu.VMEM(s, F32) for s in ((14, 8, 256), (14, 24, 256), (10, 8, 128), (10, 16, 128), (8, 16, 128))
    )
    return call(
        functools.partial(last_kernel, nx, ny),
        out_shape=shape((8, 16, 128), F32),
        in_specs=[VMEM] * 18,
        out_specs=VMEM,
        scratch_shapes=[edge] * 2 + [fine] * 2 + [thin] * 2 + [middle] * 2 + [coarse] * 4
        + [pltpu.VMEM((4, 16, 128), F32), pltpu.VMEM((2, 8, 128), F32)],
        compiler_params=limit,
        name="last",
    )(*own, al_in, ah_in, b_in, za_in, zb_in, *rows_own, ya_in, yb_in, s_in)


def solution(mesh):
    nx, ny, nz = (mesh.shape[a] for a in AXES)
    spec = P(*AXES)
    body = functools.partial(per_device, nx, ny, nz)

    return jax.shard_map(body, mesh=mesh, in_specs=(spec, spec), out_specs=spec, check_vma=False)
```

```python
import functools

import jax
import jax.numpy as jnp
from jax import lax
from jax.experimental import pallas as pl
from jax.experimental.pallas import tpu as pltpu
from jax.sharding import PartitionSpec as P


SWEEPS = 4
RELAX = 0.8
KEEP = 1.0 - RELAX
F32 = jnp.float32
VMEM = pl.BlockSpec(memory_space=pltpu.VMEM)
HIGHEST = lax.Precision.HIGHEST
AXES = ("gx", "gy", "gz")
FIRST_CHIP = 2


def along_z(chips):
    return [(i + FIRST_CHIP) % chips for i in range(chips)]


def lanes(shape=(8, 128)):
    return lax.broadcasted_iota(jnp.int32, shape, len(shape) - 1)


def rows(shape=(8, 128)):
    return lax.broadcasted_iota(jnp.int32, shape, len(shape) - 2)


def turn(x, shift, axis):
    shift = shift % x.shape[axis]
    return pltpu.roll(x, shift, axis) if shift else x


def first_kernel(
    nx, ny, in_ref, a_ref, b_ref, s_ref, v_ref, w_ref, v1_ref, w1_ref, v2_ref, w2_ref, t_ref, u_ref, d_ref,
):
    gx = lax.axis_index("gx")
    r, c = in_ref[0], in_ref[1]
    w = RELAX / (6.0 + c)
    v = w * r
    v_ref[...] = v
    w_ref[...] = w
    r4, c4 = r.reshape(4, 2, 16, 128), c.reshape(4, 2, 16, 128)
    t_ref[0:4] = r4[:, 0] + r4[:, 1]
    t_ref[4:8] = c4[:, 0] + c4[:, 1]
    a = t_ref[:, pl.ds(0, 8, stride=2), :] + t_ref[:, pl.ds(1, 8, stride=2), :]
    src, dst = rows((128, 128)), lanes((128, 128))
    half = jnp.where((src >> 1) == (dst & 63), 0.125, 0.0).astype(F32)
    one = jnp.dot(a.reshape(64, 128), half, precision=HIGHEST, preferred_element_type=F32)
    r1, c1 = one[:32].reshape(4, 8, 128), one[32:].reshape(4, 8, 128)
    d1 = RELAX / (1.5 + c1)
    v1, w1 = d1 * r1, d1 * 0.25
    v1_ref[...] = v1
    w1_ref[...] = w1
    a4 = a.reshape(4, 2, 8, 128)
    u_ref[...] = a4[:, 0] + a4[:, 1]
    e = u_ref[:, pl.ds(0, 4, stride=2), :] + u_ref[:, pl.ds(1, 4, stride=2), :]
    d_ref[:, 0:4, :] = e
    d_ref[:, 4:8, :] = e
    quarter = jnp.where((src >> 2) == (dst & 31), 0.015625, 0.0).astype(F32)
    two = jnp.dot(d_ref[...].reshape(32, 128), quarter, precision=HIGHEST, preferred_element_type=F32)
    r2, c2 = two[:16].reshape(2, 8, 128), two[16:].reshape(2, 8, 128)
    d2 = RELAX / (0.375 + c2)
    v2, w2 = d2 * r2, d2 * 0.0625
    v2_ref[...] = v2
    w2_ref[...] = w2
    lane, row = lanes(), rows()
    low = lane < 64
    sums = jnp.where(low, r2[0] + r2[1], c2[0] + c2[1])
    sums = 0.5 * jnp.sum(sums, axis=0, keepdims=True)
    quad = (lane & 63) < 32
    both = [jnp.where(quad, v2[i], w2[i]) for i in (0, 1)]
    last = jnp.where(row < 4, both[0], both[1])
    ends = [jnp.sum(jnp.where((lane >> 5) == row, v2[i], 0.0), axis=0, keepdims=True) for i in (0, 1)]
    mails = []
    for j in range(nx):
        mails.append(jnp.concatenate([sums, jnp.where(j > gx, ends[1], ends[0])], axis=0))
    for i, z in enumerate(along_z(nx * ny // 2)):
        for core in (1, 0):
            s_ref[2 * i + 1 - core] = mails[2 * (z // ny) + core]
    even = (gx & 1) == 0
    for x_ref, up in ((a_ref, even), (b_ref, jnp.logical_not(even))):
        for d in range(3):
            face = jnp.where(up, v[7 - d], v[d])
            x_ref[2 * d] = face[0:8]
            x_ref[2 * d + 1] = face[8:16]
        for d in range(2):
            face = jnp.where(up, w[7 - d], w[d])
            x_ref[6 + 2 * d] = face[0:8]
            x_ref[7 + 2 * d] = face[8:16]
        for d in range(3):
            x_ref[10 + d] = jnp.where(low, jnp.where(up, v1[3 - d], v1[d]), jnp.where(up, w1[3 - d], w1[d]))
        x_ref[13] = last


def extended(gx, v_ref, w_ref, v1_ref, w1_ref, v2_ref, w2_ref, al_ref, ah_ref, b_ref, far=(None, None)):
    lane, row = lanes(), rows()
    low = lane < 64
    quad = (lane & 63) < 32
    even = (gx & 1) == 0
    near = lambda tile: al_ref[tile] + ah_ref[tile]
    left = lambda tile: jnp.where(even, b_ref[tile], near(tile))
    right = lambda tile: jnp.where(even, near(tile), b_ref[tile])

    def pair(side, tile):
        return jnp.concatenate([side(tile), side(tile + 1)], axis=0)

    def fine(side, d):
        return pair(side, 2 * d), (pair(side, 6 + 2 * d) if d < 2 else None)

    def middle(side, d):
        t = side(10 + d)
        s = turn(t, 64, 1)
        return jnp.where(low, t, s), jnp.where(low, s, t)

    def coarse(side, layer):
        t = side(13)
        s = turn(t, 4, 0)
        t = jnp.where(row < 4, t, s) if layer == 0 else jnp.where(row < 4, s, t)
        s = turn(t, 32, 1)
        return jnp.where(quad, t, s), jnp.where(quad, s, t)

    level0 = (
        [fine(left, d) for d in (2, 1, 0)]
        + [(v_ref[i], w_ref[i]) for i in range(8)]
        + [fine(right, d) for d in (0, 1, 2)]
    )
    level1 = (
        [middle(left, d) for d in (2, 1, 0)]
        + [(v1_ref[i], w1_ref[i]) for i in range(4)]
        + [middle(right, d) for d in (0, 1, 2)]
    )
    level2 = (
        [(far[0], None), coarse(left, 0), coarse(left, 1)]
        + [(v2_ref[i], w2_ref[i]) for i in range(2)]
        + [coarse(right, 0), coarse(right, 1), (far[1], None)]
    )
    return level0, level1, level2


def edge_lanes(layers):
    shape = layers[0][0].shape
    lane = lanes(shape)
    packed = jnp.zeros(shape, F32)
    for k, (v, w) in enumerate(layers):
        at = 10 * k
        packed = jnp.where((lane >= at) & (lane < at + 6), turn(v, at + 3, 1), packed)
        packed = jnp.where((lane >= at + 6) & (lane < at + 10), turn(w, at + 8, 1), packed)
    return packed


def second_kernel(v_ref, w_ref, v1_ref, w1_ref, v2_ref, w2_ref, al_ref, ah_ref, b_ref, z_ref):
    level0, level1, level2 = extended(
        lax.axis_index("gx"), v_ref, w_ref, v1_ref, w1_ref, v2_ref, w2_ref, al_ref, ah_ref, b_ref
    )
    ends = edge_lanes(level0[1:13])
    for i, tile in enumerate((ends[0:8], ends[8:16], edge_lanes(level1[1:9]), edge_lanes(level2[1:7]))):
        z_ref[i] = tile


def faces_kernel(v_ref, w_ref, v1_ref, w1_ref, v2_ref, w2_ref, al_ref, ah_ref, b_ref, ya_ref, yb_ref):
    gx, gy = lax.axis_index("gx"), lax.axis_index("gy")
    level0, level1, level2 = extended(gx, v_ref, w_ref, v1_ref, w1_ref, v2_ref, w2_ref, al_ref, ah_ref, b_ref)
    lane, row = lanes(), rows()
    low = lane < 64
    quad = (lane & 63) < 32
    up = (gy & 1) == 0
    for k in range(12):
        v, w = level0[k + 1]
        if k < 8:
            a, b = level1[k + 1]
            extra = jnp.where(low, a, b)
        elif k < 11:
            a, b = (jnp.where(quad, *level2[1 + 2 * (k - 8) + i]) for i in (0, 1))
            extra = jnp.where(low, a, b)
        else:
            extra = jnp.zeros((8, 128), F32)
        high = jnp.where(row >= 5, v[8:16], jnp.where(row >= 3, turn(w[8:16], 5, 0), turn(extra, 3, 0)))
        base = jnp.where(row < 3, v[0:8], jnp.where(row < 5, turn(w[0:8], 3, 0), turn(extra, 5, 0)))
        ya_ref[k] = jnp.where(up, high, base)
        yb_ref[k] = jnp.where(up, base, high)


def both_ends(i, za_ref, zb_ref):
    lane = lanes()
    part = lane - 10 * (lane // 10)
    ahead = (lax.axis_index("gz") & 1) == 0
    last = (part < 3) | ((part >= 6) & (part < 8))
    from_a = jnp.where(ahead, jnp.where(last, 0, 1), jnp.where(last, 1, 0)) == 1
    return jnp.where(from_a, za_ref[i], zb_ref[i])


def third_kernel(za_ref, zb_ref, ya_ref, yb_ref, ya_out, yb_out):
    ya_out[0:12] = ya_ref[...]
    yb_out[0:12] = yb_ref[...]
    for i in range(4):
        ends = both_ends(i, za_ref, zb_ref)
        ya_out[12 + i] = ends
        yb_out[12 + i] = ends


def around(v, above, below):
    return (
        above
        + below
        + turn(v, 1, 0)
        + turn(v, -1, 0)
        + turn(v, 1, 1)
        + turn(v, -1, 1)
    )


def relaxed(start, weight, a_ref, b_ref, count):
    done = []
    for sweep in range(SWEEPS - 1):
        source = (start, lambda i: a_ref[i], lambda i: b_ref[i])[sweep]
        target = (a_ref, b_ref, None)[sweep]
        for i in range(sweep + 1, count - sweep - 1):
            v = source(i)
            new = KEEP * v + start(i) + weight(i) * around(v, source(i - 1), source(i + 1))
            if target is None:
                done.append(new)
            else:
                target[i] = new
    return done


def fourth_kernel(
    v_ref, w_ref, v1_ref, w1_ref, v2_ref, w2_ref, al_ref, ah_ref, b_ref, za_ref, zb_ref, fv, fw, mv, mw
):
    level0, level1, _ = extended(
        lax.axis_index("gx"), v_ref, w_ref, v1_ref, w1_ref, v2_ref, w2_ref, al_ref, ah_ref, b_ref
    )
    own = [both_ends(i, za_ref, zb_ref) for i in range(3)]
    z0, lane = jnp.concatenate(own[0:2], axis=0), lanes()
    for i in range(14):
        v, w = level0[i]
        fv[i, :, 0:128] = v
        if 1 <= i < 13:
            fw[i, :, 0:128] = w
            fv[i, :, 128:256] = turn(z0, -(10 * i - 7), 1)
            fw[i, :, 128:256] = turn(z0, -(10 * i - 2), 1)
        else:
            fv[i, :, 128:256] = jnp.zeros((16, 128), F32)
    for i in range(10):
        if 1 <= i < 9:
            for field, target, at in ((0, mv, 10 * i - 7), (1, mw, 10 * i - 2)):
                ends = jnp.where(lane < 96, turn(own[2], 64 - at, 1), turn(own[2], -at, 1))
                target[i] = jnp.where(lane < 64, level1[i][field], ends)
        else:
            mv[i] = level1[i][0]


def last_kernel(
    nx, ny, v_ref, w_ref, v1_ref, w1_ref, v2_ref, w2_ref, al_ref, ah_ref, b_ref, za_ref, zb_ref,
    fv_ref, fw_ref, mv_ref, mw_ref, ya_ref, yb_ref, s_ref, out_ref,
    fv, fw, fa, fb, mv, mw, ma, mb, cv, cw, ca, cb, wide_ref, deep_ref,
):
    gx, gy = lax.axis_index("gx"), lax.axis_index("gy")
    up = (gy & 1) == 0
    lane, row = lanes(), rows()

    def far(slot, have):
        chips = nx * ny // 2
        place = lax.rem((slot >> 1) * ny + gy + chips - FIRST_CHIP, chips)
        t = jnp.broadcast_to(s_ref[2 * place + 1 - (slot & 1), 1:2], (8, 128))
        spread = jnp.zeros((8, 128), F32)
        for i in range(4):
            spread = jnp.where(row == i, turn(t, -32 * i, 1), spread)
        return jnp.where(have, spread, 0.0)

    outer_layers = far(jnp.maximum(gx - 2, 0), gx > 1), far(jnp.minimum(gx + 2, nx - 1), gx < nx - 2)
    _, _, level2 = extended(
        gx, v_ref, w_ref, v1_ref, w1_ref, v2_ref, w2_ref, al_ref, ah_ref, b_ref, outer_layers
    )

    def sides(k):
        a, b = ya_ref[k], yb_ref[k]
        return jnp.where(up, a, b), jnp.where(up, b, a)

    own = both_ends(3, za_ref, zb_ref)
    plus, minus = zip(*(sides(12 + i) for i in range(4)))
    none = jnp.zeros((8, 128), F32)

    def outer(p, m):
        return jnp.where(row < 3, p, jnp.where(row >= 5, m, none))

    z0 = outer(plus[0], minus[1])
    z1 = outer(plus[2], minus[2])
    z2 = jnp.concatenate([jnp.where(row < 4, own, plus[3]), jnp.where(row >= 5, minus[3], none)], axis=0)

    lane16 = lanes((16, 128))
    for i in (0, 13):
        fv[i] = jnp.zeros((8, 256), F32)
    for i in (0, 9):
        mv[i] = none
    for k in range(12):
        p, m = sides(k)
        fv[k + 1, :, 0:128] = outer(p, m)
        fw[k + 1, :, 0:128] = jnp.where(row < 2, turn(p, 5, 0), jnp.where(row >= 6, turn(m, 3, 0), none))
        fv[k + 1, :, 128:256] = turn(z0, -(10 * k + 3), 1)
        fw[k + 1, :, 128:256] = turn(z0, -(10 * k + 8), 1)
        if k < 8:
            extra = outer(turn(p, 3, 0), turn(m, 5, 0))
            for field, target, at in ((extra, mv, 10 * k + 3), (turn(extra, 64, 1), mw, 10 * k + 8)):
                ends = jnp.where(lane < 96, turn(z1, 64 - at, 1), turn(z1, -at, 1))
                target[k + 1] = jnp.where(lane < 64, field, ends)
        elif k < 11:
            near, far = turn(p, 7, 0), turn(m, 5, 0)
            for i in (0, 1):
                j = 2 * (k - 8) + i
                v, w = level2[j + 1]
                for field, target in ((0, cv), (1, cw)):
                    shift = -(64 * i + 32 * field)
                    top = jnp.where(row < 4, (v, w)[field], turn(near, shift, 1))
                    full = jnp.concatenate([top, jnp.where(row >= 5, turn(far, shift, 1), none)], axis=0)
                    at = 10 * j + (3, 8)[field]
                    ends = jnp.where(lane16 < 64, turn(z2, 32 - at, 1), turn(z2, -at, 1))
                    target[j + 1] = jnp.where(lane16 < 32, full, ends)
    for i in (0, 7):
        cv[i, 0:8] = level2[i][0]
        cv[i, 8:16] = none

    joined = lambda near_ref, far_ref: lambda i: jnp.concatenate([near_ref[i], far_ref[i]], axis=0)
    coarse = relaxed(lambda i: cv[i], lambda i: cw[i], ca, cb, 8)
    s = jnp.sum(s_ref[...], axis=0)[0:1]
    plane = jnp.where(lane < 64, s / (turn(jnp.broadcast_to(s, (8, 128)), 64, 1) + 16.0), 0.0)
    src, dst = rows((128, 128)), lanes((128, 128))
    spread4 = jnp.where(src == (dst >> 2), 1.0, 0.0).astype(F32)
    spread2 = jnp.where(src == (dst >> 1), 1.0, 0.0).astype(F32)
    c = jnp.concatenate([layer[0:8] + plane for layer in coarse], axis=0)
    c = jnp.dot(c, spread4, precision=HIGHEST, preferred_element_type=F32).reshape(2, 8, 128)
    middle = relaxed(joined(mv_ref, mv), joined(mw_ref, mw), ma, mb, 10)
    m = jnp.concatenate([layer[0:8] for layer in middle], axis=0)
    m = jnp.dot(m, spread2, precision=HIGHEST, preferred_element_type=F32).reshape(4, 8, 128)
    for i in range(2):
        for j in range(2):
            deep_ref[i, pl.ds(j, 4, stride=2), :] = c[i, 0:4]
    for i in range(4):
        total = m[i] + deep_ref[i // 2]
        for j in range(2):
            wide_ref[i, pl.ds(j, 8, stride=2), :] = total
    fine = relaxed(joined(fv_ref, fv), joined(fw_ref, fw), fa, fb, 14)
    for i in range(8):
        out_ref[i] = fine[i][0:16, 0:128] + wide_ref[i // 2]


def per_device(nx, ny, nz, right_side, coefficient):
    shape = jax.ShapeDtypeStruct
    call = pl.pallas_call
    kept = [shape((8, 16, 128), F32)] * 2 + [shape((4, 8, 128), F32)] * 2 + [shape((2, 8, 128), F32)] * 2
    a_out, b_out, s_out, *own = call(
        functools.partial(first_kernel, nx, ny),
        out_shape=[shape((14, 8, 128), F32)] * 2 + [shape((nx * ny, 2, 128), F32)] + kept,
        in_specs=[VMEM],
        out_specs=[VMEM] * 9,
        scratch_shapes=[pltpu.VMEM(s, F32) for s in ((8, 16, 128), (4, 8, 128), (4, 8, 128))],
        compiler_params=pltpu.CompilerParams(vmem_limit_bytes=8 << 20),
        name="first",
    )(jnp.stack([right_side, coefficient]))
    even = lambda n: [(i, i ^ 1) for i in range(n)]
    odd = lambda n: [(i, i + 1 if i & 1 else i - 1) for i in range(1, n - 1)]
    al_in = lax.ppermute(a_out, "gx", even(nx)[: nx // 2])
    b_in = lax.ppermute(b_out, "gx", odd(nx))
    ring = [(2 * (z // ny) + core) * ny + z % ny for z in along_z(nx * ny // 2) for core in (1, 0)]
    s_in = lax.all_to_all(s_out, ("gx", "gy"), 0, 0, tiled=True, axis_index_groups=[ring])
    ah_in = lax.ppermute(a_out, "gx", even(nx)[nx // 2 :])
    limit = pltpu.CompilerParams(vmem_limit_bytes=8 << 20)
    z_out = call(
        second_kernel,
        out_shape=shape((4, 8, 128), F32),
        in_specs=[VMEM] * 9,
        out_specs=VMEM,
        compiler_params=limit,
        name="second",
    )(*own, al_in, ah_in, b_in)
    ya_own, yb_own = call(
        faces_kernel,
        out_shape=[shape((12, 8, 128), F32)] * 2,
        in_specs=[VMEM] * 9,
        out_specs=[VMEM] * 2,
        compiler_params=limit,
        name="faces",
    )(*own, al_in, ah_in, b_in)
    zb_in = lax.ppermute(z_out, "gz", odd(nz))
    za_in = lax.ppermute(z_out, "gz", even(nz))
    ya_out, yb_out = call(
        third_kernel,
        out_shape=[shape((16, 8, 128), F32)] * 2,
        in_specs=[VMEM] * 4,
        out_specs=[VMEM] * 2,
        compiler_params=limit,
        name="third",
    )(za_in, zb_in, ya_own, yb_own)
    yb_in = lax.ppermute(yb_out, "gy", odd(ny))
    ya_in = lax.ppermute(ya_out, "gy", even(ny))
    rows_own = call(
        fourth_kernel,
        out_shape=[shape((14, 16, 256), F32)] * 2 + [shape((10, 8, 128), F32)] * 2,
        in_specs=[VMEM] * 11,
        out_specs=[VMEM] * 4,
        compiler_params=limit,
        name="fourth",
    )(*own, al_in, ah_in, b_in, za_in, zb_in)
    edge, fine, thin, middle, coarse = (
        pltpu.VMEM(s, F32) for s in ((14, 8, 256), (14, 24, 256), (10, 8, 128), (10, 16, 128), (8, 16, 128))
    )
    return call(
        functools.partial(last_kernel, nx, ny),
        out_shape=shape((8, 16, 128), F32),
        in_specs=[VMEM] * 18,
        out_specs=VMEM,
        scratch_shapes=[edge] * 2 + [fine] * 2 + [thin] * 2 + [middle] * 2 + [coarse] * 4
        + [pltpu.VMEM((4, 16, 128), F32), pltpu.VMEM((2, 8, 128), F32)],
        compiler_params=limit,
        name="last",
    )(*own, al_in, ah_in, b_in, za_in, zb_in, *rows_own, ya_in, yb_in, s_in)


def solution(mesh):
    nx, ny, nz = (mesh.shape[a] for a in AXES)
    spec = P(*AXES)
    body = functools.partial(per_device, nx, ny, nz)

    return jax.shard_map(body, mesh=mesh, in_specs=(spec, spec), out_specs=spec, check_vma=False)
```

```python
import functools

import jax
import jax.numpy as jnp
from jax import lax
from jax.experimental import pallas as pl
from jax.experimental.pallas import tpu as pltpu
from jax.sharding import PartitionSpec as P


SWEEPS = 4
RELAX = 0.8
KEEP = 1.0 - RELAX
F32 = jnp.float32
VMEM = pl.BlockSpec(memory_space=pltpu.VMEM)
HIGHEST = lax.Precision.HIGHEST
AXES = ("gx", "gy", "gz")
FIRST_CHIP = 2


def along_z(chips):
    return [(i + FIRST_CHIP) % chips for i in range(chips)]


def lanes(shape=(8, 128)):
    return lax.broadcasted_iota(jnp.int32, shape, len(shape) - 1)


def rows(shape=(8, 128)):
    return lax.broadcasted_iota(jnp.int32, shape, len(shape) - 2)


def turn(x, shift, axis):
    shift = shift % x.shape[axis]
    return pltpu.roll(x, shift, axis) if shift else x


def first_kernel(
    nx, ny, in_ref, a_ref, b_ref, s_ref, v_ref, w_ref, v1_ref, w1_ref, v2_ref, w2_ref, t_ref, u_ref, d_ref,
):
    gx = lax.axis_index("gx")
    r, c = in_ref[0], in_ref[1]
    w = RELAX / (6.0 + c)
    v = w * r
    v_ref[...] = v
    w_ref[...] = w
    r4, c4 = r.reshape(4, 2, 16, 128), c.reshape(4, 2, 16, 128)
    t_ref[0:4] = r4[:, 0] + r4[:, 1]
    t_ref[4:8] = c4[:, 0] + c4[:, 1]
    a = t_ref[:, pl.ds(0, 8, stride=2), :] + t_ref[:, pl.ds(1, 8, stride=2), :]
    src, dst = rows((128, 128)), lanes((128, 128))
    half = jnp.where((src >> 1) == (dst & 63), 0.125, 0.0).astype(F32)
    one = jnp.dot(a.reshape(64, 128), half, precision=HIGHEST, preferred_element_type=F32)
    r1, c1 = one[:32].reshape(4, 8, 128), one[32:].reshape(4, 8, 128)
    d1 = RELAX / (1.5 + c1)
    v1, w1 = d1 * r1, d1 * 0.25
    v1_ref[...] = v1
    w1_ref[...] = w1
    a4 = a.reshape(4, 2, 8, 128)
    u_ref[...] = a4[:, 0] + a4[:, 1]
    e = u_ref[:, pl.ds(0, 4, stride=2), :] + u_ref[:, pl.ds(1, 4, stride=2), :]
    d_ref[:, 0:4, :] = e
    d_ref[:, 4:8, :] = e
    quarter = jnp.where((src >> 2) == (dst & 31), 0.015625, 0.0).astype(F32)
    two = jnp.dot(d_ref[...].reshape(32, 128), quarter, precision=HIGHEST, preferred_element_type=F32)
    r2, c2 = two[:16].reshape(2, 8, 128), two[16:].reshape(2, 8, 128)
    d2 = RELAX / (0.375 + c2)
    v2, w2 = d2 * r2, d2 * 0.0625
    v2_ref[...] = v2
    w2_ref[...] = w2
    lane, row = lanes(), rows()
    low = lane < 64
    sums = jnp.where(low, r2[0] + r2[1], c2[0] + c2[1])
    sums = 0.5 * jnp.sum(sums, axis=0, keepdims=True)
    quad = (lane & 63) < 32
    both = [jnp.where(quad, v2[i], w2[i]) for i in (0, 1)]
    last = jnp.where(row < 4, both[0], both[1])
    ends = [jnp.sum(jnp.where((lane >> 5) == row, v2[i], 0.0), axis=0, keepdims=True) for i in (0, 1)]
    mails = []
    for j in range(nx):
        mails.append(jnp.concatenate([sums, jnp.where(j > gx, ends[1], ends[0])], axis=0))
    for i, z in enumerate(along_z(nx * ny // 2)):
        for core in (1, 0):
            s_ref[2 * i + 1 - core] = mails[2 * (z // ny) + core]
    even = (gx & 1) == 0
    for x_ref, up in ((a_ref, even), (b_ref, jnp.logical_not(even))):
        for d in range(3):
            face = jnp.where(up, v[7 - d], v[d])
            x_ref[2 * d] = face[0:8]
            x_ref[2 * d + 1] = face[8:16]
        for d in range(2):
            face = jnp.where(up, w[7 - d], w[d])
            x_ref[6 + 2 * d] = face[0:8]
            x_ref[7 + 2 * d] = face[8:16]
        for d in range(3):
            x_ref[10 + d] = jnp.where(low, jnp.where(up, v1[3 - d], v1[d]), jnp.where(up, w1[3 - d], w1[d]))
        x_ref[13] = last


def extended(gx, v_ref, w_ref, v1_ref, w1_ref, v2_ref, w2_ref, al_ref, ah_ref, b_ref, far=(None, None)):
    lane, row = lanes(), rows()
    low = lane < 64
    quad = (lane & 63) < 32
    even = (gx & 1) == 0
    near = lambda tile: al_ref[tile] + ah_ref[tile]
    left = lambda tile: jnp.where(even, b_ref[tile], near(tile))
    right = lambda tile: jnp.where(even, near(tile), b_ref[tile])

    def pair(side, tile):
        return jnp.concatenate([side(tile), side(tile + 1)], axis=0)

    def fine(side, d):
        return pair(side, 2 * d), (pair(side, 6 + 2 * d) if d < 2 else None)

    def middle(side, d):
        t = side(10 + d)
        s = turn(t, 64, 1)
        return jnp.where(low, t, s), jnp.where(low, s, t)

    def coarse(side, layer):
        t = side(13)
        s = turn(t, 4, 0)
        t = jnp.where(row < 4, t, s) if layer == 0 else jnp.where(row < 4, s, t)
        s = turn(t, 32, 1)
        return jnp.where(quad, t, s), jnp.where(quad, s, t)

    level0 = (
        [fine(left, d) for d in (2, 1, 0)]
        + [(v_ref[i], w_ref[i]) for i in range(8)]
        + [fine(right, d) for d in (0, 1, 2)]
    )
    level1 = (
        [middle(left, d) for d in (2, 1, 0)]
        + [(v1_ref[i], w1_ref[i]) for i in range(4)]
        + [middle(right, d) for d in (0, 1, 2)]
    )
    level2 = (
        [(far[0], None), coarse(left, 0), coarse(left, 1)]
        + [(v2_ref[i], w2_ref[i]) for i in range(2)]
        + [coarse(right, 0), coarse(right, 1), (far[1], None)]
    )
    return level0, level1, level2


def edge_lanes(layers):
    shape = layers[0][0].shape
    lane = lanes(shape)
    packed = jnp.zeros(shape, F32)
    for k, (v, w) in enumerate(layers):
        at = 10 * k
        packed = jnp.where((lane >= at) & (lane < at + 6), turn(v, at + 3, 1), packed)
        packed = jnp.where((lane >= at + 6) & (lane < at + 10), turn(w, at + 8, 1), packed)
    return packed


def second_kernel(v_ref, w_ref, v1_ref, w1_ref, v2_ref, w2_ref, al_ref, ah_ref, b_ref, z_ref, ya_ref, yb_ref):
    gx, gy = lax.axis_index("gx"), lax.axis_index("gy")
    level0, level1, level2 = extended(gx, v_ref, w_ref, v1_ref, w1_ref, v2_ref, w2_ref, al_ref, ah_ref, b_ref)
    lane, row = lanes(), rows()
    low = lane < 64
    quad = (lane & 63) < 32
    up = (gy & 1) == 0
    ends = edge_lanes(level0[1:13])
    for i, tile in enumerate((ends[0:8], ends[8:16], edge_lanes(level1[1:9]), edge_lanes(level2[1:7]))):
        z_ref[i] = tile
    for k in range(12):
        v, w = level0[k + 1]
        if k < 8:
            a, b = level1[k + 1]
            extra = jnp.where(low, a, b)
        elif k < 11:
            a, b = (jnp.where(quad, *level2[1 + 2 * (k - 8) + i]) for i in (0, 1))
            extra = jnp.where(low, a, b)
        else:
            extra = jnp.zeros((8, 128), F32)
        high = jnp.where(row >= 5, v[8:16], jnp.where(row >= 3, turn(w[8:16], 5, 0), turn(extra, 3, 0)))
        base = jnp.where(row < 3, v[0:8], jnp.where(row < 5, turn(w[0:8], 3, 0), turn(extra, 5, 0)))
        ya_ref[k] = jnp.where(up, high, base)
        yb_ref[k] = jnp.where(up, base, high)


def both_ends(i, za_ref, zb_ref):
    lane = lanes()
    part = lane - 10 * (lane // 10)
    ahead = (lax.axis_index("gz") & 1) == 0
    last = (part < 3) | ((part >= 6) & (part < 8))
    from_a = jnp.where(ahead, jnp.where(last, 0, 1), jnp.where(last, 1, 0)) == 1
    return jnp.where(from_a, za_ref[i], zb_ref[i])


def third_kernel(za_ref, zb_ref, ya_ref, yb_ref, ya_out, yb_out):
    ya_out[0:12] = ya_ref[...]
    yb_out[0:12] = yb_ref[...]
    for i in range(4):
        ends = both_ends(i, za_ref, zb_ref)
        ya_out[12 + i] = ends
        yb_out[12 + i] = ends


def around(v, above, below):
    return (
        above
        + below
        + turn(v, 1, 0)
        + turn(v, -1, 0)
        + turn(v, 1, 1)
        + turn(v, -1, 1)
    )


def relaxed(start, weight, a_ref, b_ref, count):
    done = []
    for sweep in range(SWEEPS - 1):
        source = (start, lambda i: a_ref[i], lambda i: b_ref[i])[sweep]
        target = (a_ref, b_ref, None)[sweep]
        for i in range(sweep + 1, count - sweep - 1):
            v = source(i)
            new = KEEP * v + start(i) + weight(i) * around(v, source(i - 1), source(i + 1))
            if target is None:
                done.append(new)
            else:
                target[i] = new
    return done


def fourth_kernel(
    nx, ny, v_ref, w_ref, v1_ref, w1_ref, v2_ref, w2_ref, al_ref, ah_ref, b_ref, za_ref, zb_ref, s_ref,
    fv, fw, mv, mw, cv, cw, plane_ref,
):
    gx, gy = lax.axis_index("gx"), lax.axis_index("gy")
    row = rows()

    def far(slot, have):
        chips = nx * ny // 2
        place = lax.rem((slot >> 1) * ny + gy + chips - FIRST_CHIP, chips)
        t = jnp.broadcast_to(s_ref[2 * place + 1 - (slot & 1), 1:2], (8, 128))
        spread = jnp.zeros((8, 128), F32)
        for i in range(4):
            spread = jnp.where(row == i, turn(t, -32 * i, 1), spread)
        return jnp.where(have, spread, 0.0)

    outer_layers = far(jnp.maximum(gx - 2, 0), gx > 1), far(jnp.minimum(gx + 2, nx - 1), gx < nx - 2)
    level0, level1, level2 = extended(
        gx, v_ref, w_ref, v1_ref, w1_ref, v2_ref, w2_ref, al_ref, ah_ref, b_ref, outer_layers
    )
    for i in range(8):
        cv[i] = level2[i][0]
        if 1 <= i < 7:
            cw[i] = level2[i][1]
    s = jnp.sum(s_ref[...], axis=0)[0:1]
    plane_ref[...] = jnp.where(lanes() < 64, s / (turn(jnp.broadcast_to(s, (8, 128)), 64, 1) + 16.0), 0.0)
    own = [both_ends(i, za_ref, zb_ref) for i in range(3)]
    z0, lane = jnp.concatenate(own[0:2], axis=0), lanes()
    for i in range(14):
        v, w = level0[i]
        fv[i, :, 0:128] = v
        if 1 <= i < 13:
            fw[i, :, 0:128] = w
            fv[i, :, 128:256] = turn(z0, -(10 * i - 7), 1)
            fw[i, :, 128:256] = turn(z0, -(10 * i - 2), 1)
        else:
            fv[i, :, 128:256] = jnp.zeros((16, 128), F32)
    for i in range(10):
        if 1 <= i < 9:
            for field, target, at in ((0, mv, 10 * i - 7), (1, mw, 10 * i - 2)):
                ends = jnp.where(lane < 96, turn(own[2], 64 - at, 1), turn(own[2], -at, 1))
                target[i] = jnp.where(lane < 64, level1[i][field], ends)
        else:
            mv[i] = level1[i][0]


def last_kernel(
    za_ref, zb_ref, fv_ref, fw_ref, mv_ref, mw_ref, cv_ref, cw_ref, plane_ref, ya_ref, yb_ref, out_ref,
    fv, fw, fa, fb, mv, mw, ma, mb, cv, cw, ca, cb, wide_ref, deep_ref,
):
    up = (lax.axis_index("gy") & 1) == 0
    lane, row = lanes(), rows()

    def sides(k):
        a, b = ya_ref[k], yb_ref[k]
        return jnp.where(up, a, b), jnp.where(up, b, a)

    own = both_ends(3, za_ref, zb_ref)
    plus, minus = zip(*(sides(12 + i) for i in range(4)))
    none = jnp.zeros((8, 128), F32)

    def outer(p, m):
        return jnp.where(row < 3, p, jnp.where(row >= 5, m, none))

    z0 = outer(plus[0], minus[1])
    z1 = outer(plus[2], minus[2])
    z2 = jnp.concatenate([jnp.where(row < 4, own, plus[3]), jnp.where(row >= 5, minus[3], none)], axis=0)

    lane16 = lanes((16, 128))
    for i in (0, 13):
        fv[i] = jnp.zeros((8, 256), F32)
    for i in (0, 9):
        mv[i] = none
    for k in range(12):
        p, m = sides(k)
        fv[k + 1, :, 0:128] = outer(p, m)
        fw[k + 1, :, 0:128] = jnp.where(row < 2, turn(p, 5, 0), jnp.where(row >= 6, turn(m, 3, 0), none))
        fv[k + 1, :, 128:256] = turn(z0, -(10 * k + 3), 1)
        fw[k + 1, :, 128:256] = turn(z0, -(10 * k + 8), 1)
        if k < 8:
            extra = outer(turn(p, 3, 0), turn(m, 5, 0))
            for field, target, at in ((extra, mv, 10 * k + 3), (turn(extra, 64, 1), mw, 10 * k + 8)):
                ends = jnp.where(lane < 96, turn(z1, 64 - at, 1), turn(z1, -at, 1))
                target[k + 1] = jnp.where(lane < 64, field, ends)
        elif k < 11:
            near, far = turn(p, 7, 0), turn(m, 5, 0)
            for i in (0, 1):
                j = 2 * (k - 8) + i
                v, w = cv_ref[j + 1], cw_ref[j + 1]
                for field, target in ((0, cv), (1, cw)):
                    shift = -(64 * i + 32 * field)
                    top = jnp.where(row < 4, (v, w)[field], turn(near, shift, 1))
                    full = jnp.concatenate([top, jnp.where(row >= 5, turn(far, shift, 1), none)], axis=0)
                    at = 10 * j + (3, 8)[field]
                    ends = jnp.where(lane16 < 64, turn(z2, 32 - at, 1), turn(z2, -at, 1))
                    target[j + 1] = jnp.where(lane16 < 32, full, ends)
    for i in (0, 7):
        cv[i, 0:8] = cv_ref[i]
        cv[i, 8:16] = none

    joined = lambda near_ref, far_ref: lambda i: jnp.concatenate([near_ref[i], far_ref[i]], axis=0)
    coarse = relaxed(lambda i: cv[i], lambda i: cw[i], ca, cb, 8)
    src, dst = rows((128, 128)), lanes((128, 128))
    spread4 = jnp.where(src == (dst >> 2), 1.0, 0.0).astype(F32)
    spread2 = jnp.where(src == (dst >> 1), 1.0, 0.0).astype(F32)
    c = jnp.concatenate([layer[0:8] + plane_ref[...] for layer in coarse], axis=0)
    c = jnp.dot(c, spread4, precision=HIGHEST, preferred_element_type=F32).reshape(2, 8, 128)
    middle = relaxed(joined(mv_ref, mv), joined(mw_ref, mw), ma, mb, 10)
    m = jnp.concatenate([layer[0:8] for layer in middle], axis=0)
    m = jnp.dot(m, spread2, precision=HIGHEST, preferred_element_type=F32).reshape(4, 8, 128)
    for i in range(2):
        for j in range(2):
            deep_ref[i, pl.ds(j, 4, stride=2), :] = c[i, 0:4]
    for i in range(4):
        total = m[i] + deep_ref[i // 2]
        for j in range(2):
            wide_ref[i, pl.ds(j, 8, stride=2), :] = total
    fine = relaxed(joined(fv_ref, fv), joined(fw_ref, fw), fa, fb, 14)
    for i in range(8):
        out_ref[i] = fine[i][0:16, 0:128] + wide_ref[i // 2]


def per_device(nx, ny, nz, right_side, coefficient):
    shape = jax.ShapeDtypeStruct
    call = pl.pallas_call
    kept = [shape((8, 16, 128), F32)] * 2 + [shape((4, 8, 128), F32)] * 2 + [shape((2, 8, 128), F32)] * 2
    a_out, b_out, s_out, *own = call(
        functools.partial(first_kernel, nx, ny),
        out_shape=[shape((14, 8, 128), F32)] * 2 + [shape((nx * ny, 2, 128), F32)] + kept,
        in_specs=[VMEM],
        out_specs=[VMEM] * 9,
        scratch_shapes=[pltpu.VMEM(s, F32) for s in ((8, 16, 128), (4, 8, 128), (4, 8, 128))],
        compiler_params=pltpu.CompilerParams(vmem_limit_bytes=8 << 20),
        name="first",
    )(jnp.stack([right_side, coefficient]))
    even = lambda n: [(i, i ^ 1) for i in range(n)]
    odd = lambda n: [(i, i + 1 if i & 1 else i - 1) for i in range(1, n - 1)]
    al_in = lax.ppermute(a_out, "gx", even(nx)[: nx // 2])
    b_in = lax.ppermute(b_out, "gx", odd(nx))
    ring = [(2 * (z // ny) + core) * ny + z % ny for z in along_z(nx * ny // 2) for core in (1, 0)]
    s_in = lax.all_to_all(s_out, ("gx", "gy"), 0, 0, tiled=True, axis_index_groups=[ring])
    ah_in = lax.ppermute(a_out, "gx", even(nx)[nx // 2 :])
    limit = pltpu.CompilerParams(vmem_limit_bytes=8 << 20)
    z_out, ya_own, yb_own = call(
        second_kernel,
        out_shape=[shape((4, 8, 128), F32)] + [shape((12, 8, 128), F32)] * 2,
        in_specs=[VMEM] * 9,
        out_specs=[VMEM] * 3,
        compiler_params=limit,
        name="second",
    )(*own, al_in, ah_in, b_in)
    zb_in = lax.ppermute(z_out, "gz", odd(nz))
    za_in = lax.ppermute(z_out, "gz", even(nz))
    ya_out, yb_out = call(
        third_kernel,
        out_shape=[shape((16, 8, 128), F32)] * 2,
        in_specs=[VMEM] * 4,
        out_specs=[VMEM] * 2,
        compiler_params=limit,
        name="third",
    )(za_in, zb_in, ya_own, yb_own)
    yb_in = lax.ppermute(yb_out, "gy", odd(ny))
    ya_in = lax.ppermute(ya_out, "gy", even(ny))
    rows_own = call(
        functools.partial(fourth_kernel, nx, ny),
        out_shape=[shape((14, 16, 256), F32)] * 2 + [shape((10, 8, 128), F32)] * 2
        + [shape((8, 8, 128), F32)] * 2 + [shape((8, 128), F32)],
        in_specs=[VMEM] * 12,
        out_specs=[VMEM] * 7,
        compiler_params=limit,
        name="fourth",
    )(*own, al_in, ah_in, b_in, za_in, zb_in, s_in)
    edge, fine, thin, middle, coarse = (
        pltpu.VMEM(s, F32) for s in ((14, 8, 256), (14, 24, 256), (10, 8, 128), (10, 16, 128), (8, 16, 128))
    )
    return call(
        last_kernel,
        out_shape=shape((8, 16, 128), F32),
        in_specs=[VMEM] * 11,
        out_specs=VMEM,
        scratch_shapes=[edge] * 2 + [fine] * 2 + [thin] * 2 + [middle] * 2 + [coarse] * 4
        + [pltpu.VMEM((4, 16, 128), F32), pltpu.VMEM((2, 8, 128), F32)],
        compiler_params=limit,
        name="last",
    )(za_in, zb_in, *rows_own, ya_in, yb_in)


def solution(mesh):
    nx, ny, nz = (mesh.shape[a] for a in AXES)
    spec = P(*AXES)
    body = functools.partial(per_device, nx, ny, nz)

    return jax.shard_map(body, mesh=mesh, in_specs=(spec, spec), out_specs=spec, check_vma=False)
```

```python
import functools

import jax
import jax.numpy as jnp
from jax import lax
from jax.experimental import pallas as pl
from jax.experimental.pallas import tpu as pltpu
from jax.sharding import PartitionSpec as P


SWEEPS = 4
RELAX = 0.8
KEEP = 1.0 - RELAX
F32 = jnp.float32
VMEM = pl.BlockSpec(memory_space=pltpu.VMEM)
HIGHEST = lax.Precision.HIGHEST
AXES = ("gx", "gy", "gz")
FIRST_CHIP = 2


def along_z(chips):
    return [(i + FIRST_CHIP) % chips for i in range(chips)]


def lanes(shape=(8, 128)):
    return lax.broadcasted_iota(jnp.int32, shape, len(shape) - 1)


def rows(shape=(8, 128)):
    return lax.broadcasted_iota(jnp.int32, shape, len(shape) - 2)


def turn(x, shift, axis):
    shift = shift % x.shape[axis]
    return pltpu.roll(x, shift, axis) if shift else x


def first_kernel(
    nx, ny, in_ref, a_ref, b_ref, s_ref, v_ref, w_ref, v1_ref, w1_ref, v2_ref, w2_ref, t_ref, u_ref, d_ref,
):
    gx = lax.axis_index("gx")
    r, c = in_ref[0], in_ref[1]
    w = RELAX / (6.0 + c)
    v = w * r
    v_ref[...] = v
    w_ref[...] = w
    r4, c4 = r.reshape(4, 2, 16, 128), c.reshape(4, 2, 16, 128)
    t_ref[0:4] = r4[:, 0] + r4[:, 1]
    t_ref[4:8] = c4[:, 0] + c4[:, 1]
    a = t_ref[:, pl.ds(0, 8, stride=2), :] + t_ref[:, pl.ds(1, 8, stride=2), :]
    src, dst = rows((128, 128)), lanes((128, 128))
    half = jnp.where((src >> 1) == (dst & 63), 0.125, 0.0).astype(F32)
    one = jnp.dot(a.reshape(64, 128), half, precision=HIGHEST, preferred_element_type=F32)
    r1, c1 = one[:32].reshape(4, 8, 128), one[32:].reshape(4, 8, 128)
    d1 = RELAX / (1.5 + c1)
    v1, w1 = d1 * r1, d1 * 0.25
    v1_ref[...] = v1
    w1_ref[...] = w1
    a4 = a.reshape(4, 2, 8, 128)
    u_ref[...] = a4[:, 0] + a4[:, 1]
    e = u_ref[:, pl.ds(0, 4, stride=2), :] + u_ref[:, pl.ds(1, 4, stride=2), :]
    d_ref[:, 0:4, :] = e
    d_ref[:, 4:8, :] = e
    quarter = jnp.where((src >> 2) == (dst & 31), 0.015625, 0.0).astype(F32)
    two = jnp.dot(d_ref[...].reshape(32, 128), quarter, precision=HIGHEST, preferred_element_type=F32)
    r2, c2 = two[:16].reshape(2, 8, 128), two[16:].reshape(2, 8, 128)
    d2 = RELAX / (0.375 + c2)
    v2, w2 = d2 * r2, d2 * 0.0625
    v2_ref[...] = v2
    w2_ref[...] = w2
    lane, row = lanes(), rows()
    low = lane < 64
    sums = jnp.where(low, r2[0] + r2[1], c2[0] + c2[1])
    sums = 0.5 * jnp.sum(sums, axis=0, keepdims=True)
    quad = (lane & 63) < 32
    both = [jnp.where(quad, v2[i], w2[i]) for i in (0, 1)]
    last = jnp.where(row < 4, both[0], both[1])
    ends = [jnp.sum(jnp.where((lane >> 5) == row, v2[i], 0.0), axis=0, keepdims=True) for i in (0, 1)]
    mails = []
    for j in range(nx):
        mails.append(jnp.concatenate([sums, jnp.where(j > gx, ends[1], ends[0])], axis=0))
    for i, z in enumerate(along_z(nx * ny // 2)):
        for core in (1, 0):
            s_ref[2 * i + 1 - core] = mails[2 * (z // ny) + core]
    even = (gx & 1) == 0
    for x_ref, up in ((a_ref, even), (b_ref, jnp.logical_not(even))):
        for d in range(3):
            face = jnp.where(up, v[7 - d], v[d])
            x_ref[2 * d] = face[0:8]
            x_ref[2 * d + 1] = face[8:16]
        for d in range(2):
            face = jnp.where(up, w[7 - d], w[d])
            x_ref[6 + 2 * d] = face[0:8]
            x_ref[7 + 2 * d] = face[8:16]
        for d in range(3):
            x_ref[10 + d] = jnp.where(low, jnp.where(up, v1[3 - d], v1[d]), jnp.where(up, w1[3 - d], w1[d]))
        x_ref[13] = last


def extended(gx, v_ref, w_ref, v1_ref, w1_ref, v2_ref, w2_ref, al_ref, ah_ref, b_ref, far=(None, None)):
    lane, row = lanes(), rows()
    low = lane < 64
    quad = (lane & 63) < 32
    even = (gx & 1) == 0
    near = lambda tile: al_ref[tile] + ah_ref[tile]
    left = lambda tile: jnp.where(even, b_ref[tile], near(tile))
    right = lambda tile: jnp.where(even, near(tile), b_ref[tile])

    def pair(side, tile):
        return jnp.concatenate([side(tile), side(tile + 1)], axis=0)

    def fine(side, d):
        return pair(side, 2 * d), (pair(side, 6 + 2 * d) if d < 2 else None)

    def middle(side, d):
        t = side(10 + d)
        s = turn(t, 64, 1)
        return jnp.where(low, t, s), jnp.where(low, s, t)

    def coarse(side, layer):
        t = side(13)
        s = turn(t, 4, 0)
        t = jnp.where(row < 4, t, s) if layer == 0 else jnp.where(row < 4, s, t)
        s = turn(t, 32, 1)
        return jnp.where(quad, t, s), jnp.where(quad, s, t)

    level0 = (
        [fine(left, d) for d in (2, 1, 0)]
        + [(v_ref[i], w_ref[i]) for i in range(8)]
        + [fine(right, d) for d in (0, 1, 2)]
    )
    level1 = (
        [middle(left, d) for d in (2, 1, 0)]
        + [(v1_ref[i], w1_ref[i]) for i in range(4)]
        + [middle(right, d) for d in (0, 1, 2)]
    )
    level2 = (
        [(far[0], None), coarse(left, 0), coarse(left, 1)]
        + [(v2_ref[i], w2_ref[i]) for i in range(2)]
        + [coarse(right, 0), coarse(right, 1), (far[1], None)]
    )
    return level0, level1, level2


def edge_lanes(layers):
    shape = layers[0][0].shape
    lane = lanes(shape)
    packed = jnp.zeros(shape, F32)
    for k, (v, w) in enumerate(layers):
        at = 10 * k
        packed = jnp.where((lane >= at) & (lane < at + 6), turn(v, at + 3, 1), packed)
        packed = jnp.where((lane >= at + 6) & (lane < at + 10), turn(w, at + 8, 1), packed)
    return packed


def second_kernel(v_ref, w_ref, v1_ref, w1_ref, v2_ref, w2_ref, al_ref, ah_ref, b_ref, z_ref):
    level0, level1, level2 = extended(
        lax.axis_index("gx"), v_ref, w_ref, v1_ref, w1_ref, v2_ref, w2_ref, al_ref, ah_ref, b_ref
    )
    ends = edge_lanes(level0[1:13])
    for i, tile in enumerate((ends[0:8], ends[8:16], edge_lanes(level1[1:9]), edge_lanes(level2[1:7]))):
        z_ref[i] = tile


def faces_kernel(v_ref, w_ref, v1_ref, w1_ref, v2_ref, w2_ref, al_ref, ah_ref, b_ref, ya_ref, yb_ref):
    gx, gy = lax.axis_index("gx"), lax.axis_index("gy")
    level0, level1, level2 = extended(gx, v_ref, w_ref, v1_ref, w1_ref, v2_ref, w2_ref, al_ref, ah_ref, b_ref)
    lane, row = lanes(), rows()
    low = lane < 64
    quad = (lane & 63) < 32
    up = (gy & 1) == 0
    for k in range(12):
        v, w = level0[k + 1]
        if k < 8:
            a, b = level1[k + 1]
            extra = jnp.where(low, a, b)
        elif k < 11:
            a, b = (jnp.where(quad, *level2[1 + 2 * (k - 8) + i]) for i in (0, 1))
            extra = jnp.where(low, a, b)
        else:
            extra = jnp.zeros((8, 128), F32)
        high = jnp.where(row >= 5, v[8:16], jnp.where(row >= 3, turn(w[8:16], 5, 0), turn(extra, 3, 0)))
        base = jnp.where(row < 3, v[0:8], jnp.where(row < 5, turn(w[0:8], 3, 0), turn(extra, 5, 0)))
        ya_ref[k] = jnp.where(up, high, base)
        yb_ref[k] = jnp.where(up, base, high)


def both_ends(i, za_ref, zb_ref):
    lane = lanes()
    part = lane - 10 * (lane // 10)
    ahead = (lax.axis_index("gz") & 1) == 0
    last = (part < 3) | ((part >= 6) & (part < 8))
    from_a = jnp.where(ahead, jnp.where(last, 0, 1), jnp.where(last, 1, 0)) == 1
    return jnp.where(from_a, za_ref[i], zb_ref[i])


def third_kernel(za_ref, zb_ref, ya_ref, yb_ref, ya_out, yb_out):
    ya_out[0:12] = ya_ref[...]
    yb_out[0:12] = yb_ref[...]
    for i in range(4):
        ends = both_ends(i, za_ref, zb_ref)
        ya_out[12 + i] = ends
        yb_out[12 + i] = ends


def around(v, above, below):
    return (
        above
        + below
        + turn(v, 1, 0)
        + turn(v, -1, 0)
        + turn(v, 1, 1)
        + turn(v, -1, 1)
    )


def relaxed(start, weight, a_ref, b_ref, count):
    done = []
    for sweep in range(SWEEPS - 1):
        source = (start, lambda i: a_ref[i], lambda i: b_ref[i])[sweep]
        target = (a_ref, b_ref, None)[sweep]
        for i in range(sweep + 1, count - sweep - 1):
            v = source(i)
            new = KEEP * v + start(i) + weight(i) * around(v, source(i - 1), source(i + 1))
            if target is None:
                done.append(new)
            else:
                target[i] = new
    return done


def fourth_kernel(
    nx, ny, v_ref, w_ref, v1_ref, w1_ref, v2_ref, w2_ref, al_ref, ah_ref, b_ref, za_ref, zb_ref, s_ref,
    fv, fw, mv, mw, cv, cw, plane_ref,
):
    gx, gy = lax.axis_index("gx"), lax.axis_index("gy")
    row = rows()

    def far(slot, have):
        chips = nx * ny // 2
        place = lax.rem((slot >> 1) * ny + gy + chips - FIRST_CHIP, chips)
        t = jnp.broadcast_to(s_ref[2 * place + 1 - (slot & 1), 1:2], (8, 128))
        spread = jnp.zeros((8, 128), F32)
        for i in range(4):
            spread = jnp.where(row == i, turn(t, -32 * i, 1), spread)
        return jnp.where(have, spread, 0.0)

    outer_layers = far(jnp.maximum(gx - 2, 0), gx > 1), far(jnp.minimum(gx + 2, nx - 1), gx < nx - 2)
    level0, level1, level2 = extended(
        gx, v_ref, w_ref, v1_ref, w1_ref, v2_ref, w2_ref, al_ref, ah_ref, b_ref, outer_layers
    )
    for i in range(8):
        cv[i] = level2[i][0]
        if 1 <= i < 7:
            cw[i] = level2[i][1]
    s = jnp.sum(s_ref[...], axis=0)[0:1]
    plane_ref[...] = jnp.where(lanes() < 64, s / (turn(jnp.broadcast_to(s, (8, 128)), 64, 1) + 16.0), 0.0)
    own = [both_ends(i, za_ref, zb_ref) for i in range(3)]
    z0, lane = jnp.concatenate(own[0:2], axis=0), lanes()
    for i in range(14):
        v, w = level0[i]
        fv[i, :, 0:128] = v
        if 1 <= i < 13:
            fw[i, :, 0:128] = w
            fv[i, :, 128:256] = turn(z0, -(10 * i - 7), 1)
            fw[i, :, 128:256] = turn(z0, -(10 * i - 2), 1)
        else:
            fv[i, :, 128:256] = jnp.zeros((16, 128), F32)
    for i in range(10):
        if 1 <= i < 9:
            for field, target, at in ((0, mv, 10 * i - 7), (1, mw, 10 * i - 2)):
                ends = jnp.where(lane < 96, turn(own[2], 64 - at, 1), turn(own[2], -at, 1))
                target[i] = jnp.where(lane < 64, level1[i][field], ends)
        else:
            mv[i] = level1[i][0]


def last_kernel(
    za_ref, zb_ref, fv_ref, fw_ref, mv_ref, mw_ref, cv_ref, cw_ref, plane_ref, ya_ref, yb_ref, out_ref,
    fv, fw, fa, fb, mv, mw, ma, mb, cv, cw, ca, cb, wide_ref, deep_ref,
):
    up = (lax.axis_index("gy") & 1) == 0
    lane, row = lanes(), rows()

    def sides(k):
        a, b = ya_ref[k], yb_ref[k]
        return jnp.where(up, a, b), jnp.where(up, b, a)

    own = both_ends(3, za_ref, zb_ref)
    plus, minus = zip(*(sides(12 + i) for i in range(4)))
    none = jnp.zeros((8, 128), F32)

    def outer(p, m):
        return jnp.where(row < 3, p, jnp.where(row >= 5, m, none))

    z0 = outer(plus[0], minus[1])
    z1 = outer(plus[2], minus[2])
    z2 = jnp.concatenate([jnp.where(row < 4, own, plus[3]), jnp.where(row >= 5, minus[3], none)], axis=0)

    lane16 = lanes((16, 128))
    for i in (0, 13):
        fv[i] = jnp.zeros((8, 256), F32)
    for i in (0, 9):
        mv[i] = none
    for k in range(12):
        p, m = sides(k)
        fv[k + 1, :, 0:128] = outer(p, m)
        fw[k + 1, :, 0:128] = jnp.where(row < 2, turn(p, 5, 0), jnp.where(row >= 6, turn(m, 3, 0), none))
        fv[k + 1, :, 128:256] = turn(z0, -(10 * k + 3), 1)
        fw[k + 1, :, 128:256] = turn(z0, -(10 * k + 8), 1)
        if k < 8:
            extra = outer(turn(p, 3, 0), turn(m, 5, 0))
            for field, target, at in ((extra, mv, 10 * k + 3), (turn(extra, 64, 1), mw, 10 * k + 8)):
                ends = jnp.where(lane < 96, turn(z1, 64 - at, 1), turn(z1, -at, 1))
                target[k + 1] = jnp.where(lane < 64, field, ends)
        elif k < 11:
            near, far = turn(p, 7, 0), turn(m, 5, 0)
            for i in (0, 1):
                j = 2 * (k - 8) + i
                v, w = cv_ref[j + 1], cw_ref[j + 1]
                for field, target in ((0, cv), (1, cw)):
                    shift = -(64 * i + 32 * field)
                    top = jnp.where(row < 4, (v, w)[field], turn(near, shift, 1))
                    full = jnp.concatenate([top, jnp.where(row >= 5, turn(far, shift, 1), none)], axis=0)
                    at = 10 * j + (3, 8)[field]
                    ends = jnp.where(lane16 < 64, turn(z2, 32 - at, 1), turn(z2, -at, 1))
                    target[j + 1] = jnp.where(lane16 < 32, full, ends)
    for i in (0, 7):
        cv[i, 0:8] = cv_ref[i]
        cv[i, 8:16] = none

    joined = lambda near_ref, far_ref: lambda i: jnp.concatenate([near_ref[i], far_ref[i]], axis=0)
    coarse = relaxed(lambda i: cv[i], lambda i: cw[i], ca, cb, 8)
    src, dst = rows((128, 128)), lanes((128, 128))
    spread4 = jnp.where(src == (dst >> 2), 1.0, 0.0).astype(F32)
    spread2 = jnp.where(src == (dst >> 1), 1.0, 0.0).astype(F32)
    c = jnp.concatenate([layer[0:8] + plane_ref[...] for layer in coarse], axis=0)
    c = jnp.dot(c, spread4, precision=HIGHEST, preferred_element_type=F32).reshape(2, 8, 128)
    middle = relaxed(joined(mv_ref, mv), joined(mw_ref, mw), ma, mb, 10)
    m = jnp.concatenate([layer[0:8] for layer in middle], axis=0)
    m = jnp.dot(m, spread2, precision=HIGHEST, preferred_element_type=F32).reshape(4, 8, 128)
    for i in range(2):
        for j in range(2):
            deep_ref[i, pl.ds(j, 4, stride=2), :] = c[i, 0:4]
    for i in range(4):
        total = m[i] + deep_ref[i // 2]
        for j in range(2):
            wide_ref[i, pl.ds(j, 8, stride=2), :] = total
    fine = relaxed(joined(fv_ref, fv), joined(fw_ref, fw), fa, fb, 14)
    for i in range(8):
        out_ref[i] = fine[i][0:16, 0:128] + wide_ref[i // 2]


def per_device(nx, ny, nz, right_side, coefficient):
    shape = jax.ShapeDtypeStruct
    call = pl.pallas_call
    kept = [shape((8, 16, 128), F32)] * 2 + [shape((4, 8, 128), F32)] * 2 + [shape((2, 8, 128), F32)] * 2
    a_out, b_out, s_out, *own = call(
        functools.partial(first_kernel, nx, ny),
        out_shape=[shape((14, 8, 128), F32)] * 2 + [shape((nx * ny, 2, 128), F32)] + kept,
        in_specs=[VMEM],
        out_specs=[VMEM] * 9,
        scratch_shapes=[pltpu.VMEM(s, F32) for s in ((8, 16, 128), (4, 8, 128), (4, 8, 128))],
        compiler_params=pltpu.CompilerParams(vmem_limit_bytes=8 << 20),
        name="first",
    )(jnp.stack([right_side, coefficient]))
    even = lambda n: [(i, i ^ 1) for i in range(n)]
    odd = lambda n: [(i, i + 1 if i & 1 else i - 1) for i in range(1, n - 1)]
    al_in = lax.ppermute(a_out, "gx", even(nx)[: nx // 2])
    b_in = lax.ppermute(b_out, "gx", odd(nx))
    ring = [(2 * (z // ny) + core) * ny + z % ny for z in along_z(nx * ny // 2) for core in (1, 0)]
    s_in = lax.all_to_all(s_out, ("gx", "gy"), 0, 0, tiled=True, axis_index_groups=[ring])
    ah_in = lax.ppermute(a_out, "gx", even(nx)[nx // 2 :])
    limit = pltpu.CompilerParams(vmem_limit_bytes=8 << 20)
    z_out = call(
        second_kernel,
        out_shape=shape((4, 8, 128), F32),
        in_specs=[VMEM] * 9,
        out_specs=VMEM,
        compiler_params=limit,
        name="second",
    )(*own, al_in, ah_in, b_in)
    ya_own, yb_own = call(
        faces_kernel,
        out_shape=[shape((12, 8, 128), F32)] * 2,
        in_specs=[VMEM] * 9,
        out_specs=[VMEM] * 2,
        compiler_params=limit,
        name="faces",
    )(*own, al_in, ah_in, b_in)
    zb_in = lax.ppermute(z_out, "gz", odd(nz))
    za_in = lax.ppermute(z_out, "gz", even(nz))
    ya_out, yb_out = call(
        third_kernel,
        out_shape=[shape((16, 8, 128), F32)] * 2,
        in_specs=[VMEM] * 4,
        out_specs=[VMEM] * 2,
        compiler_params=limit,
        name="third",
    )(za_in, zb_in, ya_own, yb_own)
    yb_in = lax.ppermute(yb_out, "gy", odd(ny))
    ya_in = lax.ppermute(ya_out, "gy", even(ny))
    rows_own = call(
        functools.partial(fourth_kernel, nx, ny),
        out_shape=[shape((14, 16, 256), F32)] * 2 + [shape((10, 8, 128), F32)] * 2
        + [shape((8, 8, 128), F32)] * 2 + [shape((8, 128), F32)],
        in_specs=[VMEM] * 12,
        out_specs=[VMEM] * 7,
        compiler_params=limit,
        name="fourth",
    )(*own, al_in, ah_in, b_in, za_in, zb_in, s_in)
    edge, fine, thin, middle, coarse = (
        pltpu.VMEM(s, F32) for s in ((14, 8, 256), (14, 24, 256), (10, 8, 128), (10, 16, 128), (8, 16, 128))
    )
    return call(
        last_kernel,
        out_shape=shape((8, 16, 128), F32),
        in_specs=[VMEM] * 11,
        out_specs=VMEM,
        scratch_shapes=[edge] * 2 + [fine] * 2 + [thin] * 2 + [middle] * 2 + [coarse] * 4
        + [pltpu.VMEM((4, 16, 128), F32), pltpu.VMEM((2, 8, 128), F32)],
        compiler_params=limit,
        name="last",
    )(za_in, zb_in, *rows_own, ya_in, yb_in)


def solution(mesh):
    nx, ny, nz = (mesh.shape[a] for a in AXES)
    spec = P(*AXES)
    body = functools.partial(per_device, nx, ny, nz)

    return jax.shard_map(body, mesh=mesh, in_specs=(spec, spec), out_specs=spec, check_vma=False)
```
